256 devices in a mesh: tm: 8 (over y, core), chan: 32 (over z, x).
Axes of the slice: x: 4, y: 4, z: 8, core: 2. Of those that a mesh axis runs over, the one named last changes fastest.
Arguments:
- filterbank: bfloat16 [1024, 2048], P('chan', 'tm'), may hold values from -6 to 6
- chan_delay: int32 [1024], replicated, may hold values from 0 to 4096, as said below
- tail_len: int32 [128], replicated, may hold values from 1 to 256, as said below
- kernels: bfloat16 [2, 32, 256], replicated, may hold values from -0.375 to 0.375
Outputs:
- accel_power: bfloat16 [32, 128, 1024], P(None, 'chan', 'tm')
The draws below stay inside these ranges and needn't reach their ends.
Inputs may be any that keep to these rules, and one draw needn't show every extreme that they name: `chan_delay`: some channel has exactly 4096. `tail_len`: some trial has exactly 256.
All inputs are finite; a program needn't handle non-finite values.
Results may differ from the reference program's by a relative error of at most 0.011.
Values may be sent and summed in bfloat16 or wider, within the bound.
A program may use at most 64 MiB of HBM per device.

```python
import math
import jax
import jax.numpy as jnp
from jax import lax

CHANNELS = 1024
TRIAL_DEV = 4
BLOCK = 256
MAXDELAY = 4096
ACCELS = 32
TAPS = 256
TRIALS = 128
SAMPLES = 2048
N_TM = 8


def draw_chan_delay(key, part):
    value_key = jax.random.fold_in(key, 11)
    chosen_key = jax.random.fold_in(key, 12)
    values = jax.random.randint(value_key, (CHANNELS,), 0, MAXDELAY + 1, dtype=jnp.int32)
    chosen = jax.random.randint(chosen_key, (), 0, CHANNELS, dtype=jnp.int32)
    return jnp.where(jnp.arange(CHANNELS, dtype=jnp.int32) == chosen, MAXDELAY, values).astype(jnp.int32)


def draw_tail_len(key, part):
    value_key = jax.random.fold_in(key, 21)
    chosen_key = jax.random.fold_in(key, 22)
    values = jax.random.randint(value_key, (TRIALS,), 1, BLOCK + 1, dtype=jnp.int32)
    chosen = jax.random.randint(chosen_key, (), 0, TRIALS, dtype=jnp.int32)
    return jnp.where(jnp.arange(TRIALS, dtype=jnp.int32) == chosen, BLOCK, values).astype(jnp.int32)


def block_scale(stream_key, shape, shards, smallest, top_value):
    loudness = 1.0
    for dim, shards_of in shards:
        heights = jax.random.uniform(jax.random.fold_in(jax.random.fold_in(stream_key, 6), dim), (shards_of,), jnp.float32, smallest / len(shards), top_value / len(shards))
        loudness = loudness * jnp.repeat(jnp.exp(heights), shape[dim] // shards_of).reshape((-1,) + (1,) * (len(shape) - 1 - dim))
    return loudness


def gaussian(rng, dims, width, bound, cuts=(), held_as=jnp.bfloat16):
    array = width * jax.random.normal(rng, dims, jnp.float32)
    if cuts:
        array = array * block_scale(rng, dims, cuts, -0.22, 0.18)
    return jnp.clip(array, -bound, bound).astype(held_as)


def setup_inputs(seed: int = 0) -> dict:
    splits = jax.random.split(jax.random.key(seed), 5)
    return {
        "filterbank": gaussian(splits[0], (CHANNELS, SAMPLES), 1.0, 6.0, ((0, 32), (1, 8))),
        "chan_delay": draw_chan_delay(jax.random.fold_in(splits[4], 71), 0),
        "tail_len": draw_tail_len(jax.random.fold_in(splits[4], 71), 0),
        "kernels": gaussian(splits[3], (2, ACCELS, TAPS), TAPS ** -0.5, 0.375),
    }


def forward_table(block_len):
    period = 2 * block_len
    sample_idx = jnp.arange(block_len, dtype=jnp.int32)
    phases = sample_idx[:, None] * sample_idx[None, :] % period
    angles = phases.astype(jnp.float32) * (2.0 * math.pi / period)
    return jnp.concatenate([jnp.cos(angles), -jnp.sin(angles)], axis=1).astype(jnp.bfloat16)

def inverse_table(block_len):
    period = 2 * block_len
    bin_index = jnp.arange(block_len, dtype=jnp.int32)
    position = jnp.arange(period, dtype=jnp.int32)
    offsets = (position + block_len) % period
    phases = bin_index[:, None] * offsets[None, :] % period
    angles = phases.astype(jnp.float32) * (2.0 * math.pi / period)
    weights = jnp.where(bin_index == 0, 1.0, 2.0).astype(jnp.bfloat16)[:, None]
    cosines = jnp.cos(angles).astype(jnp.bfloat16)
    sine_vals = jnp.sin(angles).astype(jnp.bfloat16)
    return jnp.concatenate([cosines * weights, -(sine_vals * weights)], axis=0)

def block_table(block_len):
    half_len = block_len // 2
    sample_idx = jnp.arange(block_len, dtype=jnp.int32)
    bin_index = jnp.arange(half_len, dtype=jnp.int32)
    phases = sample_idx[:, None] * bin_index[None, :] % block_len
    angles = phases.astype(jnp.float32) * (2.0 * math.pi / block_len)
    return jnp.concatenate([jnp.cos(angles), -jnp.sin(angles)], axis=1).astype(jnp.bfloat16)

def kernel_weights(kernels):
    real_kernel = kernels[0]
    imag_kernel = kernels[1]
    upper_rows = jnp.stack([real_kernel, -imag_kernel], axis=1)
    lower_rows = jnp.stack([imag_kernel, real_kernel], axis=1)
    return jnp.concatenate([upper_rows, lower_rows], axis=0)

def correlate(block_spectra, weights, tap_count):
    return lax.conv_general_dilated(block_spectra, weights, (1,), [(tap_count // 2, tap_count - 1 - tap_count // 2)], preferred_element_type=jnp.float32)

def reference(filterbank, chan_delay, tail_len, kernels):
    block_len = BLOCK
    period = 2 * block_len
    half_len = block_len // 2
    forward = forward_table(block_len)
    inverse = inverse_table(block_len)
    blocked = block_table(block_len)
    shifts = chan_delay[:, None] * tail_len[None, :] // MAXDELAY
    lookup = jnp.arange(period, dtype=jnp.int32).astype(jnp.float32) * (2.0 * math.pi / period)
    cos_lookup = jnp.cos(lookup).astype(jnp.bfloat16).astype(jnp.float32)
    sin_lookup = jnp.sin(lookup).astype(jnp.bfloat16).astype(jnp.float32)
    bin_index = jnp.arange(block_len, dtype=jnp.int32)
    trial_blocks = TRIALS // TRIAL_DEV

    def one_group(group_index):
        samples = lax.dynamic_slice_in_dim(filterbank, group_index * block_len, block_len, axis=1)
        spectra = (jnp.dot(samples, forward, preferred_element_type=jnp.float32) * (1.0 / math.sqrt(block_len))).astype(jnp.bfloat16)
        real_part = spectra[:, :block_len].astype(jnp.float32)
        imag_part = spectra[:, block_len:].astype(jnp.float32)

        def trial_block(first_trial):
            part_shifts = lax.dynamic_slice_in_dim(shifts, first_trial, TRIAL_DEV, axis=1)
            phases = part_shifts[:, :, None] * bin_index[None, None, :] % period
            ramp_cos = jnp.take(cos_lookup, phases)
            ramp_sin = jnp.take(sin_lookup, phases)
            out_real = jnp.einsum('ck,cdk->dk', real_part, ramp_cos) - jnp.einsum('ck,cdk->dk', imag_part, ramp_sin)
            out_imag = jnp.einsum('ck,cdk->dk', real_part, ramp_sin) + jnp.einsum('ck,cdk->dk', imag_part, ramp_cos)
            return jnp.concatenate([out_real, out_imag], axis=1) * (1.0 / math.sqrt(CHANNELS))
        firsts = jnp.arange(trial_blocks, dtype=jnp.int32) * TRIAL_DEV
        dedispersed = lax.map(trial_block, firsts).reshape(TRIALS, 2 * block_len)
        return jnp.dot(dedispersed.astype(jnp.bfloat16), inverse, preferred_element_type=jnp.float32) * (0.5 / math.sqrt(block_len))
    block_series = lax.map(one_group, jnp.arange(N_TM, dtype=jnp.int32))
    positions = jnp.arange(block_len, dtype=jnp.int32)
    keep_mask = positions[None, :] >= block_len - tail_len[:, None]
    tail_parts = jnp.where(keep_mask[None], block_series[:, :, :block_len], 0.0)
    following = jnp.concatenate([tail_parts[1:], jnp.zeros_like(tail_parts[:1])], axis=0)
    series = (block_series[:, :, block_len:] + following).astype(jnp.bfloat16)
    spectra_blocks = (jnp.dot(series.reshape(N_TM * TRIALS, block_len), blocked, preferred_element_type=jnp.float32) * (1.0 / math.sqrt(block_len))).astype(jnp.bfloat16)
    spectra_blocks = spectra_blocks.reshape(N_TM * TRIALS, 2, half_len).astype(jnp.float32)
    weights = kernel_weights(kernels.astype(jnp.float32))
    correlation = correlate(spectra_blocks, weights, TAPS)
    power_out = correlation[:, :ACCELS] * correlation[:, :ACCELS] + correlation[:, ACCELS:] * correlation[:, ACCELS:]
    power_out = power_out.reshape(N_TM, TRIALS, ACCELS, half_len).transpose(2, 1, 0, 3).reshape(ACCELS, TRIALS, N_TM * half_len)
    return power_out.astype(jnp.bfloat16)
```

```python
import functools
import math

import jax
import jax.numpy as jnp
import ml_dtypes
import numpy as np
from jax import lax
from jax.experimental import pallas as pl
from jax.experimental.pallas import tpu as pltpu
from jax.sharding import PartitionSpec as P

MESH = pl.DeviceIdType.MESH
NZ, NX, NTM = 8, 4, 8
NCHAN = NZ * NX
F32, BF16 = jnp.float32, jnp.bfloat16
ORDER = sorted(range(NCHAN), key=lambda i: -(min(i // NX, NZ - i // NX) + min(i % NX, NX - i % NX)))


def block_table():
    t = np.arange(256)[:, None]
    k = np.arange(128)[None, :]
    angles = (t * k % 256) * (2.0 * math.pi / 256)
    table = np.concatenate([np.cos(angles), -np.sin(angles)], axis=1)
    return np.concatenate([table[:128], table[128:]], axis=1).astype(ml_dtypes.bfloat16)


def iota(shape, axis):
    return lax.broadcasted_iota(jnp.int32, shape, axis)


def kernel(
    x_ref, delay_ref, tail_ref, taps_ref, table_ref, out_ref,
    xpad, xgroup, acc, stage, send_body, send_tail, recv_body, recv_tail,
    send_sem, body_sem, tail_sem,
):
    me = lax.axis_index("chan")
    tm = lax.axis_index("tm")
    z, x_pos = me // NX, lax.rem(me, NX)

    def peer(i):
        return lax.rem(z + i // NX, NZ) * NX + lax.rem(x_pos + i % NX, NX)

    barrier = pltpu.get_barrier_semaphore()
    for i in ORDER:
        if i:
            pl.semaphore_signal(barrier, inc=1, device_id={"chan": peer(i)}, device_id_type=MESH)

    @pl.when(tm < NTM - 1)
    def _():
        for i in ORDER:
            pl.semaphore_signal(
                barrier, inc=1, device_id={"chan": peer(i), "tm": tm + 1}, device_id_type=MESH
            )

    row = delay_ref[pl.ds(me // 4, 1), :].astype(F32)
    pick = iota((32, 128), 1) == iota((32, 128), 0) + 32 * lax.rem(me, 4)
    delay = jnp.sum(jnp.where(pick, row, 0.0), axis=1, keepdims=True).astype(jnp.int32)
    tails = pltpu.roll(jnp.broadcast_to(tail_ref[...], (8, 128)), lax.rem(128 - 16 * z, 128), 1)
    lane16 = lax.rem(iota((8, 128), 1), 16)
    ahead = pltpu.roll(tails, lax.rem(128 - 4 * x_pos, 128), 1)
    behind = pltpu.roll(tails, lax.rem(16 - 4 * x_pos, 128), 1)
    tails = jnp.where(lane16 < 16 - 4 * x_pos, ahead, behind)[0:1]
    shifts = (delay * tails) >> 12
    shift_bf = shifts.astype(F32).astype(BF16)

    x = x_ref[...].astype(F32)
    xt = jnp.transpose(jnp.concatenate([x, x, x, x], axis=0))
    xpad[pl.ds(0, 16), :] = jnp.zeros((16, 128), F32)
    xpad[pl.ds(16, 256), :] = xt
    xpad[pl.ds(272, 24), :] = jnp.zeros((24, 128), F32)
    group = iota((288, 128), 1) // 32
    shifted = xpad[pl.ds(0, 288), :]
    for beta in range(1, 4):
        shifted = jnp.where(group == beta, xpad[pl.ds(beta, 288), :], shifted)
    xgroup[...] = shifted
    windows = jnp.concatenate([xgroup[pl.ds(4 * j, 272), :] for j in range(4)], axis=1).astype(BF16)

    acc[...] = jnp.zeros_like(acc)
    one, zero = jnp.ones((), BF16), jnp.zeros((), BF16)

    def one_hot(a):
        return jnp.concatenate(
            [jnp.where(shift_bf == jnp.asarray(16 * a + b, BF16), one, zero) for b in range(16)], axis=0
        )

    for pair in range(8):
        a = 2 * pair
        hot = jnp.concatenate([one_hot(a), one_hot(a + 1)], axis=1)
        part = jnp.dot(windows, hot, preferred_element_type=F32)
        acc[pl.ds(256 - 16 * a, 272), :] += part[:, :128]
        acc[pl.ds(240 - 16 * a, 272), :] += part[:, 128:]
    longest = jnp.where(shift_bf == jnp.asarray(256, BF16), one, zero)
    longest = jnp.concatenate([longest, jnp.zeros((96, 128), BF16)], axis=0)
    acc[pl.ds(0, 272), :] += jnp.dot(windows[:, :128], longest, preferred_element_type=F32)

    sign = (1 - 2 * lax.rem(iota((32, 256), 1), 2)).astype(F32)
    alternating = jnp.sum(x * sign, axis=1, keepdims=True)
    parity = (1 - 2 * (shifts & 1)).astype(F32)
    nyquist = jnp.sum(alternating * parity, axis=0, keepdims=True) * (1.0 / 512.0)
    row_sign = (1 - 2 * lax.rem(iota((128, 128), 0), 2)).astype(F32)
    for q in range(4):
        series = acc[pl.ds(16 + 128 * q, 128), :] - row_sign * nyquist
        if q < 2:
            series = jnp.where(iota((128, 128), 0) + 128 * q >= 256 - tails, series, 0.0)
        stage[:, pl.ds(4 * q, 4), :] = jnp.transpose(series).reshape(NCHAN, 4, 128)
    send_tail[...] = stage[:, 0:8, :].astype(BF16)
    send_body[...] = stage[:, 8:16, :].astype(BF16)

    def body_copy(i):
        return pltpu.make_async_remote_copy(
            send_body.at[i], recv_body.at[i], send_sem, body_sem,
            device_id={"chan": peer(i)}, device_id_type=MESH,
        )

    def tail_copy(i):
        return pltpu.make_async_remote_copy(
            send_tail.at[i], recv_tail.at[i], send_sem, tail_sem,
            device_id={"chan": peer(i), "tm": tm - 1}, device_id_type=MESH,
        )

    @pl.when(tm == 0)
    def _():
        pl.semaphore_wait(barrier, NCHAN - 1)
        for i in ORDER:
            if i:
                body_copy(i).start()

    @pl.when(tm > 0)
    def _():
        pl.semaphore_wait(barrier, 2 * NCHAN - 1)
        for i in ORDER:
            tail_copy(i).start()
            if i:
                body_copy(i).start()

    flip = (iota((128, 128), 0) + iota((128, 128), 1) == 127).astype(F32).astype(BF16)
    halves = [
        jnp.dot(taps_ref[:, pl.ds(128 * h, 128)], flip, preferred_element_type=F32) for h in range(2)
    ]
    real = jnp.concatenate([halves[0][:32], halves[1][:32]], axis=1)
    imag = jnp.concatenate([halves[0][32:], halves[1][32:]], axis=1)
    left = jnp.concatenate(
        [jnp.concatenate([real, -imag], axis=1), jnp.concatenate([imag, real], axis=1)], axis=0
    ).astype(BF16)

    recv_tail_all = pltpu.make_async_remote_copy(
        recv_tail, recv_tail, send_sem, tail_sem, device_id={"chan": peer(1)}, device_id_type=MESH
    )
    recv_body_all = pltpu.make_async_remote_copy(
        recv_body.at[pl.ds(1, NCHAN - 1)], recv_body.at[pl.ds(1, NCHAN - 1)], send_sem, body_sem,
        device_id={"chan": peer(1)}, device_id_type=MESH,
    )

    @pl.when(tm == NTM - 1)
    def _():
        recv_tail[...] = jnp.zeros_like(recv_tail)

    @pl.when(tm < NTM - 1)
    def _():
        recv_tail_all.wait_recv()

    total = jnp.sum(recv_tail[...].astype(F32), axis=0)
    recv_body_all.wait_recv()
    total = total + jnp.sum(recv_body[1:].astype(F32), axis=0) + send_body[0].astype(F32)
    series = (total * (1.0 / 32.0)).astype(BF16)
    both = jnp.dot(series, table_ref[...], preferred_element_type=F32)
    spectra = (both[0:4, 0:256] + both[4:8, 256:512]) * (1.0 / 16.0)
    spectra = spectra.astype(BF16).astype(F32)
    later = iota((128, 128), 1) > iota((128, 128), 0)
    columns = []
    for d in range(4):
        blocks = []
        for part in range(2):
            line = spectra[d : d + 1, 128 * part : 128 * part + 128]
            rolled = pltpu.roll(jnp.broadcast_to(line, (128, 128)), 1, 1, stride=1, stride_axis=0)
            blocks += [jnp.where(later, rolled, 0.0), jnp.where(later, 0.0, rolled)]
        columns.append(jnp.concatenate(blocks, axis=0).astype(BF16))
    for d in range(4):
        corr = jnp.dot(left, columns[d], preferred_element_type=F32)
        out_ref[d] = (corr[:32] * corr[:32] + corr[32:] * corr[32:]).astype(BF16)

    @pl.when(tm == 0)
    def _():
        recv_body_all.wait_send()

    @pl.when(tm > 0)
    def _():
        recv_body_all.wait_send()
        recv_tail_all.wait_send()


def shards(filterbank, chan_delay, tail_len, kernels):
    vmem = pl.BlockSpec(memory_space=pltpu.VMEM)
    power = pl.pallas_call(
        kernel,
        out_shape=jax.ShapeDtypeStruct((4, 32, 128), BF16),
        in_specs=[vmem] * 5,
        out_specs=vmem,
        scratch_shapes=[
            pltpu.VMEM((296, 128), F32),
            pltpu.VMEM((288, 128), F32),
            pltpu.VMEM((528, 128), F32),
            pltpu.VMEM((NCHAN, 16, 128), F32),
            pltpu.VMEM((NCHAN, 8, 128), BF16),
            pltpu.VMEM((NCHAN, 8, 128), BF16),
            pltpu.VMEM((NCHAN, 8, 128), BF16),
            pltpu.VMEM((NCHAN, 8, 128), BF16),
            pltpu.SemaphoreType.DMA,
            pltpu.SemaphoreType.DMA,
            pltpu.SemaphoreType.DMA,
        ],
        compiler_params=pltpu.CompilerParams(
            collective_id=0, has_side_effects=True, vmem_limit_bytes=32 * 1024 * 1024
        ),
        name="dedisperse",
    )(
        filterbank,
        chan_delay.reshape(8, 128),
        tail_len.reshape(1, 128),
        kernels.reshape(64, 256),
        jnp.asarray(block_table()),
    )
    return power.transpose(1, 0, 2)


def solution(mesh):
    placed = (P("chan", "tm"), P(), P(), P())
    return jax.shard_map(
        shards, mesh=mesh, in_specs=placed, out_specs=P(None, "chan", "tm"), check_vma=False
    )
```

```python
import functools
import math

import jax
import jax.numpy as jnp
import ml_dtypes
import numpy as np
from jax import lax
from jax.experimental import pallas as pl
from jax.experimental.pallas import tpu as pltpu
from jax.sharding import PartitionSpec as P

MESH = pl.DeviceIdType.MESH
NCHAN, NTM = 32, 8
F32, BF16 = jnp.float32, jnp.bfloat16

def block_table():
    t = np.arange(256)[:, None]
    k = np.arange(128)[None, :]
    angles = (t * k % 256) * (2.0 * math.pi / 256)
    table = np.concatenate([np.cos(angles), -np.sin(angles)], axis=1)
    return np.concatenate([table[:128], table[128:]], axis=1).astype(ml_dtypes.bfloat16)


def iota(shape, axis):
    return lax.broadcasted_iota(jnp.int32, shape, axis)


def kernel(
    x_hbm, delay_hbm, tail_hbm, taps_hbm, table_hbm, out_ref,
    x_ref, delay_ref, tail_ref, taps_ref, table_ref, load_sems, xpad, xgroup, acc, stage, send, recv, send_sem, recv_sems, ready_sem,
):
    me = lax.axis_index("chan")
    tm = lax.axis_index("tm")
    before, after = lax.rem(tm + NTM - 1, NTM), lax.rem(tm + 1, NTM)

    def other(i):
        return i + (me <= i).astype(jnp.int32)

    pairs = [
        (delay_hbm, delay_ref), (tail_hbm, tail_ref), (x_hbm, x_ref), (taps_hbm, taps_ref), (table_hbm, table_ref)
    ]
    loads = [pltpu.make_async_copy(a, b, load_sems.at[n]) for n, (a, b) in enumerate(pairs)]
    for load in loads[:3]:
        load.start()
    barrier = pltpu.get_barrier_semaphore()
    for i in reversed(range(NCHAN - 1)):
        pl.semaphore_signal(barrier, inc=1, device_id={"chan": other(i)}, device_id_type=MESH)

    @pl.when(tm > 0)
    def _():
        pl.semaphore_signal(barrier, inc=1, device_id={"tm": before}, device_id_type=MESH)

    for load in loads[3:]:
        load.start()

    loads[0].wait()
    loads[1].wait()
    row = delay_ref[pl.ds(me // 4, 1), :].astype(F32)
    pick = iota((32, 128), 1) == iota((32, 128), 0) + 32 * lax.rem(me, 4)
    delay = jnp.sum(jnp.where(pick, row, 0.0), axis=1, keepdims=True).astype(jnp.int32)
    tails = jnp.broadcast_to(tail_ref[...], (8, 128))
    lane = iota((8, 128), 1)
    turned = pltpu.roll(tails, 64, 1)
    tails = [jnp.where(lane < 64, tails, turned)[0:1], jnp.where(lane < 64, turned, tails)[0:1]]

    loads[2].wait()
    x = x_ref[...].astype(F32)
    xt = jnp.transpose(jnp.concatenate([x, x, x, x], axis=0))
    xpad[pl.ds(0, 16), :] = jnp.zeros((16, 128), F32)
    xpad[pl.ds(16, 256), :] = xt
    xpad[pl.ds(272, 24), :] = jnp.zeros((24, 128), F32)
    group = iota((288, 128), 1) // 32
    shifted = xpad[pl.ds(0, 288), :]
    for beta in range(1, 4):
        shifted = jnp.where(group == beta, xpad[pl.ds(beta, 288), :], shifted)
    xgroup[...] = shifted
    windows = jnp.concatenate([xgroup[pl.ds(4 * j, 272), :] for j in range(4)], axis=1).astype(BF16)
    sign = (1 - 2 * lax.rem(iota((32, 256), 1), 2)).astype(F32)
    alternating = jnp.sum(x * sign, axis=1, keepdims=True)
    row_sign = (1 - 2 * lax.rem(iota((128, 128), 0), 2)).astype(F32)
    one, zero = jnp.ones((), BF16), jnp.zeros((), BF16)

    def copy_to(kind, p):
        return pltpu.make_async_remote_copy(
            send.at[kind, p], recv.at[kind, me], send_sem, recv_sems.at[kind],
            device_id={"chan": p, "tm": tm if kind else before}, device_id_type=MESH,
        )

    for half in range(2):
        shifts = (delay * tails[half]) >> 12
        shift_bf = (shifts - 16 * (iota((32, 128), 1) // 64)).astype(F32).astype(BF16)

        def one_hot(a):
            return jnp.concatenate(
                [jnp.where(shift_bf == jnp.asarray(32 * a + b, BF16), one, zero) for b in range(16)], axis=0
            )

        acc[...] = jnp.zeros_like(acc)
        for pair in range(4):
            a = 2 * pair
            hot = jnp.concatenate([one_hot(a), one_hot(a + 1)], axis=1)
            part = jnp.dot(windows, hot, preferred_element_type=F32)
            acc[pl.ds(256 - 32 * a, 272), :] += part[:, :128]
            acc[pl.ds(224 - 32 * a, 272), :] += part[:, 128:]
        longest = jnp.where(shift_bf == jnp.asarray(256, BF16), one, zero)
        longest = jnp.concatenate([longest, jnp.zeros((96, 128), BF16)], axis=0)
        acc[pl.ds(0, 272), :] += jnp.dot(windows[:, :128], longest, preferred_element_type=F32)

        parity = (1 - 2 * (shifts & 1)).astype(F32)
        nyquist = jnp.sum(alternating * parity, axis=0, keepdims=True) * (1.0 / 512.0)
        slots = pl.ds(16 * half, 16)
        for q in range(4):
            odd = pltpu.roll(acc[pl.ds(32 + 128 * q, 128), :], 64, 1)
            series = acc[pl.ds(16 + 128 * q, 128), :] + odd - row_sign * nyquist
            if q < 2:
                series = jnp.where(iota((128, 128), 0) + 128 * q >= 256 - tails[half], series, 0.0)
            stage[:, pl.ds(4 * q, 4), :] = jnp.transpose(series)[:64].reshape(16, 4, 128)
        send[0, slots] = stage[:, 0:8, :].astype(BF16)
        send[1, slots] = stage[:, 8:16, :].astype(BF16)

    def send_bodies():
        for i in range(NCHAN - 1):
            copy_to(1, other(i)).start()

    pl.semaphore_wait(barrier, NCHAN - 1 + (2 * NTM - 2 - tm) // NTM)

    @pl.when(tm < NTM - 1)
    def _():
        pl.semaphore_signal(ready_sem, inc=1, device_id={"tm": after}, device_id_type=MESH)

    pl.when(lax.rem(tm, 2) == 1)(send_bodies)

    @pl.when(tm > 0)
    def _():
        pl.semaphore_wait(ready_sem, 1)
        for p in range(NCHAN):
            copy_to(0, p).start()

    pl.when(lax.rem(tm, 2) == 0)(send_bodies)

    loads[3].wait()
    loads[4].wait()
    flip = (iota((128, 128), 0) + iota((128, 128), 1) == 127).astype(F32).astype(BF16)
    halves = [
        jnp.dot(taps_ref[:, pl.ds(128 * h, 128)], flip, preferred_element_type=F32) for h in range(2)
    ]
    real = jnp.concatenate([halves[0][:32], halves[1][:32]], axis=1)
    imag = jnp.concatenate([halves[0][32:], halves[1][32:]], axis=1)
    left = jnp.concatenate(
        [jnp.concatenate([real, -imag], axis=1), jnp.concatenate([imag, real], axis=1)], axis=0
    ).astype(BF16)
    recv[1, me] = send[1, me]

    def arrived(kind, count):
        there = recv.at[kind, pl.ds(0, count)]
        return pltpu.make_async_remote_copy(
            there, there, send_sem, recv_sems.at[kind], device_id={"chan": other(0)}, device_id_type=MESH
        )

    tail_all, body_all = arrived(0, NCHAN), arrived(1, NCHAN - 1)
    @pl.when(tm == NTM - 1)
    def _():
        recv[0] = jnp.zeros_like(recv[0])

    body_all.wait_recv()

    @pl.when(tm < NTM - 1)
    def _():
        tail_all.wait_recv()

    total = jnp.sum(recv[0].astype(F32), axis=0) + jnp.sum(recv[1].astype(F32), axis=0)
    series = (total * (1.0 / 32.0)).astype(BF16)
    both = jnp.dot(series, table_ref[...], preferred_element_type=F32)
    spectra = (both[0:4, 0:256] + both[4:8, 256:512]) * (1.0 / 16.0)
    spectra = spectra.astype(BF16).astype(F32)
    later = iota((128, 128), 1) > iota((128, 128), 0)
    columns = []
    for d in range(4):
        blocks = []
        for part in range(2):
            line = spectra[d : d + 1, 128 * part : 128 * part + 128]
            rolled = pltpu.roll(jnp.broadcast_to(line, (128, 128)), 1, 1, stride=1, stride_axis=0)
            blocks += [jnp.where(later, rolled, 0.0), jnp.where(later, 0.0, rolled)]
        columns.append(jnp.concatenate(blocks, axis=0).astype(BF16))
    for d in range(4):
        corr = jnp.dot(left, columns[d], preferred_element_type=F32)
        out_ref[d] = (corr[:32] * corr[:32] + corr[32:] * corr[32:]).astype(BF16)
    body_all.wait_send()

    @pl.when(tm > 0)
    def _():
        tail_all.wait_send()


def shards(filterbank, chan_delay, tail_len, kernels):
    vmem = pl.BlockSpec(memory_space=pltpu.VMEM)
    power = pl.pallas_call(
        kernel,
        out_shape=jax.ShapeDtypeStruct((4, 32, 128), BF16),
        in_specs=[pl.BlockSpec(memory_space=pltpu.HBM)] * 5,
        out_specs=vmem,
        scratch_shapes=[
            pltpu.VMEM((32, 256), BF16),
            pltpu.VMEM((8, 128), jnp.int32),
            pltpu.VMEM((1, 128), jnp.int32),
            pltpu.VMEM((64, 256), BF16),
            pltpu.VMEM((128, 512), BF16),
            pltpu.SemaphoreType.DMA((5,)),
            pltpu.VMEM((296, 128), F32),
            pltpu.VMEM((288, 128), F32),
            pltpu.VMEM((544, 128), F32),
            pltpu.VMEM((16, 16, 128), F32),
            pltpu.VMEM((2, NCHAN, 8, 128), BF16),
            pltpu.VMEM((2, NCHAN, 8, 128), BF16),
            pltpu.SemaphoreType.DMA,
            pltpu.SemaphoreType.DMA((2,)),
            pltpu.SemaphoreType.REGULAR,
        ],
        compiler_params=pltpu.CompilerParams(
            collective_id=0, has_side_effects=True, vmem_limit_bytes=32 * 1024 * 1024
        ),
        name="dedisperse",
    )(
        *[
            pltpu.with_memory_space_constraint(a, pltpu.HBM)
            for a in (
                filterbank,
                chan_delay.reshape(8, 128),
                tail_len.reshape(1, 128),
                kernels.reshape(64, 256),
                jnp.asarray(block_table()),
            )
        ]
    )
    return power.transpose(1, 0, 2)


def solution(mesh):
    placed = (P("chan", "tm"), P(), P(), P())
    return jax.shard_map(
        shards, mesh=mesh, in_specs=placed, out_specs=P(None, "chan", "tm"), check_vma=False
    )
```

```python
import functools
import math

import jax
import jax.numpy as jnp
import ml_dtypes
import numpy as np
from jax import lax
from jax.experimental import pallas as pl
from jax.experimental.pallas import tpu as pltpu
from jax.sharding import PartitionSpec as P

MESH = pl.DeviceIdType.MESH
NCHAN, NTM = 32, 8
F32, BF16 = jnp.float32, jnp.bfloat16

def block_table():
    t = np.arange(256)[:, None]
    k = np.arange(128)[None, :]
    angles = (t * k % 256) * (2.0 * math.pi / 256)
    table = np.concatenate([np.cos(angles), -np.sin(angles)], axis=1)
    return np.concatenate([table[:128], table[128:]], axis=1).astype(ml_dtypes.bfloat16)


def iota(shape, axis):
    return lax.broadcasted_iota(jnp.int32, shape, axis)


def kernel(
    x_hbm, delay_hbm, tail_hbm, taps_hbm, table_hbm, out_ref,
    x_ref, delay_ref, tail_ref, taps_ref, table_ref, load_sems, xpad, xgroup, acc, stage, send, recv, send_sem, recv_sems, ready_sem,
):
    me = lax.axis_index("chan")
    tm = lax.axis_index("tm")
    before, after = lax.rem(tm + NTM - 1, NTM), lax.rem(tm + 1, NTM)

    def other(i):
        return i + (me <= i).astype(jnp.int32)

    pairs = [
        (delay_hbm, delay_ref), (tail_hbm, tail_ref), (x_hbm, x_ref), (taps_hbm, taps_ref), (table_hbm, table_ref)
    ]
    loads = [pltpu.make_async_copy(a, b, load_sems.at[n]) for n, (a, b) in enumerate(pairs)]
    for load in loads[:3]:
        load.start()
    barrier = pltpu.get_barrier_semaphore()

    def tell(sem, p, block):
        pl.semaphore_signal(sem, inc=1, device_id={"chan": p, "tm": block}, device_id_type=MESH)

    @pl.when(tm == 1)
    def _():
        tell(barrier, me, 0)

    @pl.when(tm < NTM - 1)
    def _():
        for p in reversed(range(NCHAN)):
            tell(barrier, p, after)

    @pl.when(tm == NTM - 1)
    def _():
        for i in reversed(range(NCHAN - 1)):
            tell(barrier, other(i), tm)

    for load in loads[3:]:
        load.start()

    loads[0].wait()
    loads[1].wait()
    row = delay_ref[pl.ds(me // 4, 1), :].astype(F32)
    pick = iota((32, 128), 1) == iota((32, 128), 0) + 32 * lax.rem(me, 4)
    delay = jnp.sum(jnp.where(pick, row, 0.0), axis=1, keepdims=True).astype(jnp.int32)
    tails = jnp.broadcast_to(tail_ref[...], (8, 128))
    lane = iota((8, 128), 1)
    turned = pltpu.roll(tails, 64, 1)
    tails = [jnp.where(lane < 64, tails, turned)[0:1], jnp.where(lane < 64, turned, tails)[0:1]]

    loads[2].wait()
    x = x_ref[...].astype(F32)
    xt = jnp.transpose(jnp.concatenate([x, x, x, x], axis=0))
    xpad[pl.ds(0, 16), :] = jnp.zeros((16, 128), F32)
    xpad[pl.ds(16, 256), :] = xt
    xpad[pl.ds(272, 24), :] = jnp.zeros((24, 128), F32)
    group = iota((288, 128), 1) // 32
    shifted = xpad[pl.ds(0, 288), :]
    for beta in range(1, 4):
        shifted = jnp.where(group == beta, xpad[pl.ds(beta, 288), :], shifted)
    xgroup[...] = shifted
    windows = jnp.concatenate([xgroup[pl.ds(4 * j, 272), :] for j in range(4)], axis=1).astype(BF16)
    sign = (1 - 2 * lax.rem(iota((32, 256), 1), 2)).astype(F32)
    alternating = jnp.sum(x * sign, axis=1, keepdims=True)
    row_sign = (1 - 2 * lax.rem(iota((128, 128), 0), 2)).astype(F32)
    one, zero = jnp.ones((), BF16), jnp.zeros((), BF16)

    def copy_to(kind, p):
        return pltpu.make_async_remote_copy(
            send.at[kind, p], recv.at[kind, me], send_sem, recv_sems.at[kind],
            device_id={"chan": p, "tm": tm if kind else before}, device_id_type=MESH,
        )

    for half in range(2):
        shifts = (delay * tails[half]) >> 12
        shift_bf = (shifts - 16 * (iota((32, 128), 1) // 64)).astype(F32).astype(BF16)

        def one_hot(a):
            return jnp.concatenate(
                [jnp.where(shift_bf == jnp.asarray(32 * a + b, BF16), one, zero) for b in range(16)], axis=0
            )

        acc[...] = jnp.zeros_like(acc)
        for pair in range(4):
            a = 2 * pair
            hot = jnp.concatenate([one_hot(a), one_hot(a + 1)], axis=1)
            part = jnp.dot(windows, hot, preferred_element_type=F32)
            acc[pl.ds(256 - 32 * a, 272), :] += part[:, :128]
            acc[pl.ds(224 - 32 * a, 272), :] += part[:, 128:]
        longest = jnp.where(shift_bf == jnp.asarray(256, BF16), one, zero)
        longest = jnp.concatenate([longest, jnp.zeros((96, 128), BF16)], axis=0)
        acc[pl.ds(0, 272), :] += jnp.dot(windows[:, :128], longest, preferred_element_type=F32)

        parity = (1 - 2 * (shifts & 1)).astype(F32)
        nyquist = jnp.sum(alternating * parity, axis=0, keepdims=True) * (1.0 / 512.0)
        slots = pl.ds(16 * half, 16)
        for q in range(4):
            odd = pltpu.roll(acc[pl.ds(32 + 128 * q, 128), :], 64, 1)
            series = acc[pl.ds(16 + 128 * q, 128), :] + odd - row_sign * nyquist
            if q < 2:
                series = jnp.where(iota((128, 128), 0) + 128 * q >= 256 - tails[half], series, 0.0)
            stage[:, pl.ds(4 * q, 4), :] = jnp.transpose(series)[:64].reshape(16, 4, 128)
        send[0, slots] = stage[:, 0:8, :].astype(BF16)
        send[1, slots] = stage[:, 8:16, :].astype(BF16)

    pl.semaphore_wait(barrier, 1 + (NCHAN - 1) * ((tm + NTM - 2) // (NTM - 1) + tm // (NTM - 1)))

    @pl.when(tm > 0)
    def _():
        tell(ready_sem, me, before)
        for p in range(NCHAN):
            copy_to(0, p).start()

    @pl.when(tm < NTM - 1)
    def _():
        pl.semaphore_wait(ready_sem, 1)

    for i in range(NCHAN - 1):
        copy_to(1, other(i)).start()

    loads[3].wait()
    loads[4].wait()
    flip = (iota((128, 128), 0) + iota((128, 128), 1) == 127).astype(F32).astype(BF16)
    halves = [
        jnp.dot(taps_ref[:, pl.ds(128 * h, 128)], flip, preferred_element_type=F32) for h in range(2)
    ]
    real = jnp.concatenate([halves[0][:32], halves[1][:32]], axis=1)
    imag = jnp.concatenate([halves[0][32:], halves[1][32:]], axis=1)
    left = jnp.concatenate(
        [jnp.concatenate([real, -imag], axis=1), jnp.concatenate([imag, real], axis=1)], axis=0
    ).astype(BF16)
    recv[1, me] = send[1, me]

    def arrived(kind, count):
        there = recv.at[kind, pl.ds(0, count)]
        return pltpu.make_async_remote_copy(
            there, there, send_sem, recv_sems.at[kind], device_id={"chan": other(0)}, device_id_type=MESH
        )

    tail_all, body_all = arrived(0, NCHAN), arrived(1, NCHAN - 1)
    @pl.when(tm == NTM - 1)
    def _():
        recv[0] = jnp.zeros_like(recv[0])

    body_all.wait_recv()

    @pl.when(tm < NTM - 1)
    def _():
        tail_all.wait_recv()

    total = jnp.sum(recv[0].astype(F32), axis=0) + jnp.sum(recv[1].astype(F32), axis=0)
    series = (total * (1.0 / 32.0)).astype(BF16)
    both = jnp.dot(series, table_ref[...], preferred_element_type=F32)
    spectra = (both[0:4, 0:256] + both[4:8, 256:512]) * (1.0 / 16.0)
    spectra = spectra.astype(BF16).astype(F32)
    later = iota((128, 128), 1) > iota((128, 128), 0)
    columns = []
    for d in range(4):
        blocks = []
        for part in range(2):
            line = spectra[d : d + 1, 128 * part : 128 * part + 128]
            rolled = pltpu.roll(jnp.broadcast_to(line, (128, 128)), 1, 1, stride=1, stride_axis=0)
            blocks += [jnp.where(later, rolled, 0.0), jnp.where(later, 0.0, rolled)]
        columns.append(jnp.concatenate(blocks, axis=0).astype(BF16))
    for d in range(4):
        corr = jnp.dot(left, columns[d], preferred_element_type=F32)
        out_ref[d] = (corr[:32] * corr[:32] + corr[32:] * corr[32:]).astype(BF16)
    body_all.wait_send()

    @pl.when(tm > 0)
    def _():
        tail_all.wait_send()


def shards(filterbank, chan_delay, tail_len, kernels):
    vmem = pl.BlockSpec(memory_space=pltpu.VMEM)
    power = pl.pallas_call(
        kernel,
        out_shape=jax.ShapeDtypeStruct((4, 32, 128), BF16),
        in_specs=[pl.BlockSpec(memory_space=pltpu.HBM)] * 5,
        out_specs=vmem,
        scratch_shapes=[
            pltpu.VMEM((32, 256), BF16),
            pltpu.VMEM((8, 128), jnp.int32),
            pltpu.VMEM((1, 128), jnp.int32),
            pltpu.VMEM((64, 256), BF16),
            pltpu.VMEM((128, 512), BF16),
            pltpu.SemaphoreType.DMA((5,)),
            pltpu.VMEM((296, 128), F32),
            pltpu.VMEM((288, 128), F32),
            pltpu.VMEM((544, 128), F32),
            pltpu.VMEM((16, 16, 128), F32),
            pltpu.VMEM((2, NCHAN, 8, 128), BF16),
            pltpu.VMEM((2, NCHAN, 8, 128), BF16),
            pltpu.SemaphoreType.DMA,
            pltpu.SemaphoreType.DMA((2,)),
            pltpu.SemaphoreType.REGULAR,
        ],
        compiler_params=pltpu.CompilerParams(
            collective_id=0, has_side_effects=True, vmem_limit_bytes=32 * 1024 * 1024
        ),
        name="dedisperse",
    )(
        *[
            pltpu.with_memory_space_constraint(a, pltpu.HBM)
            for a in (
                filterbank,
                chan_delay.reshape(8, 128),
                tail_len.reshape(1, 128),
                kernels.reshape(64, 256),
                jnp.asarray(block_table()),
            )
        ]
    )
    return power.transpose(1, 0, 2)


def solution(mesh):
    placed = (P("chan", "tm"), P(), P(), P())
    return jax.shard_map(
        shards, mesh=mesh, in_specs=placed, out_specs=P(None, "chan", "tm"), check_vma=False
    )
```

```python
import functools
import math

import jax
import jax.numpy as jnp
import ml_dtypes
import numpy as np
from jax import lax
from jax.experimental import pallas as pl
from jax.experimental.pallas import tpu as pltpu
from jax.sharding import PartitionSpec as P

MESH = pl.DeviceIdType.MESH
NCHAN, NTM, HALF = 32, 8, 16
NEAR_FIRST = list(range(HALF))
F32, BF16 = jnp.float32, jnp.bfloat16

def block_table():
    t = np.arange(256)[:, None]
    k = np.arange(128)[None, :]
    angles = (t * k % 256) * (2.0 * math.pi / 256)
    table = np.concatenate([np.cos(angles), -np.sin(angles)], axis=1)
    return np.concatenate([table[:128], table[128:]], axis=1).astype(ml_dtypes.bfloat16)


def iota(shape, axis):
    return lax.broadcasted_iota(jnp.int32, shape, axis)


def kernel(
    x_hbm, delay_hbm, tail_hbm, taps_hbm, table_hbm, out_ref,
    x_ref, delay_ref, tail_ref, taps_ref, table_ref, load_sems, xpad, xgroup, acc, stage, send, recv, send_sem, recv_sems, ready_sem, go_sem,
):
    me = lax.axis_index("chan")
    tm = lax.axis_index("tm")
    before, after = lax.rem(tm + NTM - 1, NTM), lax.rem(tm + 1, NTM)

    def other(i):
        return i + (me <= i).astype(jnp.int32)

    pairs = [
        (delay_hbm, delay_ref), (tail_hbm, tail_ref), (x_hbm, x_ref), (taps_hbm, taps_ref), (table_hbm, table_ref)
    ]
    loads = [pltpu.make_async_copy(a, b, load_sems.at[n]) for n, (a, b) in enumerate(pairs)]
    for load in loads[:3]:
        load.start()
    barrier = pltpu.get_barrier_semaphore()

    def tell(sem, p, block):
        pl.semaphore_signal(sem, inc=1, device_id={"chan": p, "tm": block}, device_id_type=MESH)

    first_half, second_half = me < HALF, me >= HALF
    second = me // HALF
    not_first = (tm + NTM - 2) // (NTM - 1)
    last = tm // (NTM - 1)

    @pl.when(first_half)
    def _():
        for p in reversed(range(HALF, NCHAN)):
            tell(barrier, p, tm)

        @pl.when(tm == 1)
        def _():
            tell(barrier, me, 0)

        @pl.when(tm < NTM - 1)
        def _():
            for p in reversed(range(NCHAN)):
                tell(barrier, p, after)

        @pl.when(tm == NTM - 1)
        def _():
            for i in range(HALF - 1):
                tell(barrier, other(i), tm)

    @pl.when(second_half)
    def _():
        for p in range(HALF):
            tell(barrier, p, lax.min(tm + 1, NTM - 1))

    for load in loads[3:]:
        load.start()

    loads[0].wait()
    loads[1].wait()
    row = delay_ref[pl.ds(me // 4, 1), :].astype(F32)
    pick = iota((32, 128), 1) == iota((32, 128), 0) + 32 * lax.rem(me, 4)
    delay = jnp.sum(jnp.where(pick, row, 0.0), axis=1, keepdims=True).astype(jnp.int32)
    tails = jnp.broadcast_to(tail_ref[...], (8, 128))
    lane = iota((8, 128), 1)
    turned = pltpu.roll(tails, 64, 1)
    tails = [jnp.where(lane < 64, tails, turned)[0:1], jnp.where(lane < 64, turned, tails)[0:1]]

    loads[2].wait()
    x = x_ref[...].astype(F32)
    xt = jnp.transpose(jnp.concatenate([x, x, x, x], axis=0))
    xpad[pl.ds(0, 16), :] = jnp.zeros((16, 128), F32)
    xpad[pl.ds(16, 256), :] = xt
    xpad[pl.ds(272, 24), :] = jnp.zeros((24, 128), F32)
    group = iota((288, 128), 1) // 32
    shifted = xpad[pl.ds(0, 288), :]
    for beta in range(1, 4):
        shifted = jnp.where(group == beta, xpad[pl.ds(beta, 288), :], shifted)
    xgroup[...] = shifted
    windows = jnp.concatenate([xgroup[pl.ds(4 * j, 272), :] for j in range(4)], axis=1).astype(BF16)
    sign = (1 - 2 * lax.rem(iota((32, 256), 1), 2)).astype(F32)
    alternating = jnp.sum(x * sign, axis=1, keepdims=True)
    row_sign = (1 - 2 * lax.rem(iota((128, 128), 0), 2)).astype(F32)
    one, zero = jnp.ones((), BF16), jnp.zeros((), BF16)

    def copy_to(kind, p):
        return pltpu.make_async_remote_copy(
            send.at[kind, p], recv.at[kind, me], send_sem, recv_sems.at[kind],
            device_id={"chan": p, "tm": tm if kind else before}, device_id_type=MESH,
        )

    def send_tails(half):
        @pl.when(tm > 0)
        def _():
            for p in range(HALF * half, HALF * half + HALF):
                copy_to(0, p).start()

    def send_bodies(half):
        for i in range(HALF - 1):
            copy_to(1, other(HALF * half + i)).start()

        @pl.when(first_half if half else second_half)
        def _():
            copy_to(1, HALF if half else HALF - 1).start()

    for half in range(2):
        shifts = (delay * tails[half]) >> 12
        shift_bf = (shifts - 16 * (iota((32, 128), 1) // 64)).astype(F32).astype(BF16)

        def one_hot(a):
            return jnp.concatenate(
                [jnp.where(shift_bf == jnp.asarray(32 * a + b, BF16), one, zero) for b in range(16)], axis=0
            )

        acc[...] = jnp.zeros_like(acc)
        for pair in range(4):
            a = 2 * pair
            hot = jnp.concatenate([one_hot(a), one_hot(a + 1)], axis=1)
            part = jnp.dot(windows, hot, preferred_element_type=F32)
            acc[pl.ds(256 - 32 * a, 272), :] += part[:, :128]
            acc[pl.ds(224 - 32 * a, 272), :] += part[:, 128:]
        longest = jnp.where(shift_bf == jnp.asarray(256, BF16), one, zero)
        longest = jnp.concatenate([longest, jnp.zeros((96, 128), BF16)], axis=0)
        acc[pl.ds(0, 272), :] += jnp.dot(windows[:, :128], longest, preferred_element_type=F32)

        parity = (1 - 2 * (shifts & 1)).astype(F32)
        nyquist = jnp.sum(alternating * parity, axis=0, keepdims=True) * (1.0 / 512.0)
        slots = pl.ds(16 * half, 16)
        for q in range(4):
            odd = pltpu.roll(acc[pl.ds(32 + 128 * q, 128), :], 64, 1)
            series = acc[pl.ds(16 + 128 * q, 128), :] + odd - row_sign * nyquist
            if q < 2:
                series = jnp.where(iota((128, 128), 0) + 128 * q >= 256 - tails[half], series, 0.0)
            stage[:, pl.ds(4 * q, 4), :] = jnp.transpose(series)[:64].reshape(16, 4, 128)
        send[0, slots] = stage[:, 0:8, :].astype(BF16)
        send[1, slots] = stage[:, 8:16, :].astype(BF16)
        if half == 0:

            @pl.when(second_half)
            def _():
                pl.semaphore_wait(barrier, HALF + HALF * not_first)

                @pl.when(tm > 0)
                def _():
                    for p in NEAR_FIRST:
                        copy_to(0, p).start()
                        copy_to(1, p).start()

                @pl.when(tm == 0)
                def _():
                    for p in NEAR_FIRST:
                        copy_to(1, p).start()


    @pl.when(first_half)
    def _():
        pl.semaphore_wait(barrier, 1 + (NCHAN - 1) * (not_first + last))

        @pl.when(tm > 0)
        def _():
            tell(ready_sem, me, before)

        send_tails(0)
        send_tails(1)

        @pl.when(tm < NTM - 1)
        def _():
            pl.semaphore_wait(ready_sem, 1)

        tell(go_sem, NCHAN - 4 - me + 2 * lax.rem(me, 4), tm)
        send_bodies(0)
        send_bodies(1)

    @pl.when(second_half)
    def _():
        pl.semaphore_wait(go_sem, 1)
        send_tails(1)
        send_bodies(1)

    loads[3].wait()
    loads[4].wait()
    flip = (iota((128, 128), 0) + iota((128, 128), 1) == 127).astype(F32).astype(BF16)
    halves = [
        jnp.dot(taps_ref[:, pl.ds(128 * h, 128)], flip, preferred_element_type=F32) for h in range(2)
    ]
    real = jnp.concatenate([halves[0][:32], halves[1][:32]], axis=1)
    imag = jnp.concatenate([halves[0][32:], halves[1][32:]], axis=1)
    left = jnp.concatenate(
        [jnp.concatenate([real, -imag], axis=1), jnp.concatenate([imag, real], axis=1)], axis=0
    ).astype(BF16)
    recv[1, me] = send[1, me]

    def arrived(kind, count):
        there = recv.at[kind, pl.ds(0, count)]
        return pltpu.make_async_remote_copy(
            there, there, send_sem, recv_sems.at[kind], device_id={"chan": other(0)}, device_id_type=MESH
        )

    tail_all, body_all = arrived(0, NCHAN), arrived(1, NCHAN - 1)
    @pl.when(tm == NTM - 1)
    def _():
        recv[0] = jnp.zeros_like(recv[0])

    body_all.wait_recv()

    @pl.when(tm < NTM - 1)
    def _():
        tail_all.wait_recv()

    total = jnp.sum(recv[0].astype(F32), axis=0) + jnp.sum(recv[1].astype(F32), axis=0)
    series = (total * (1.0 / 32.0)).astype(BF16)
    both = jnp.dot(series, table_ref[...], preferred_element_type=F32)
    spectra = (both[0:4, 0:256] + both[4:8, 256:512]) * (1.0 / 16.0)
    spectra = spectra.astype(BF16).astype(F32)
    later = iota((128, 128), 1) > iota((128, 128), 0)
    columns = []
    for d in range(4):
        blocks = []
        for part in range(2):
            line = spectra[d : d + 1, 128 * part : 128 * part + 128]
            rolled = pltpu.roll(jnp.broadcast_to(line, (128, 128)), 1, 1, stride=1, stride_axis=0)
            blocks += [jnp.where(later, rolled, 0.0), jnp.where(later, 0.0, rolled)]
        columns.append(jnp.concatenate(blocks, axis=0).astype(BF16))
    for d in range(4):
        corr = jnp.dot(left, columns[d], preferred_element_type=F32)
        out_ref[d] = (corr[:32] * corr[:32] + corr[32:] * corr[32:]).astype(BF16)
    body_all.wait_send()

    @pl.when(tm > 0)
    def _():
        tail_all.wait_send()


def shards(filterbank, chan_delay, tail_len, kernels):
    vmem = pl.BlockSpec(memory_space=pltpu.VMEM)
    power = pl.pallas_call(
        kernel,
        out_shape=jax.ShapeDtypeStruct((4, 32, 128), BF16),
        in_specs=[pl.BlockSpec(memory_space=pltpu.HBM)] * 5,
        out_specs=vmem,
        scratch_shapes=[
            pltpu.VMEM((32, 256), BF16),
            pltpu.VMEM((8, 128), jnp.int32),
            pltpu.VMEM((1, 128), jnp.int32),
            pltpu.VMEM((64, 256), BF16),
            pltpu.VMEM((128, 512), BF16),
            pltpu.SemaphoreType.DMA((5,)),
            pltpu.VMEM((296, 128), F32),
            pltpu.VMEM((288, 128), F32),
            pltpu.VMEM((544, 128), F32),
            pltpu.VMEM((16, 16, 128), F32),
            pltpu.VMEM((2, NCHAN, 8, 128), BF16),
            pltpu.VMEM((2, NCHAN, 8, 128), BF16),
            pltpu.SemaphoreType.DMA,
            pltpu.SemaphoreType.DMA((2,)),
            pltpu.SemaphoreType.REGULAR,
            pltpu.SemaphoreType.REGULAR,
        ],
        compiler_params=pltpu.CompilerParams(
            collective_id=0, has_side_effects=True, vmem_limit_bytes=32 * 1024 * 1024
        ),
        name="dedisperse",
    )(
        *[
            pltpu.with_memory_space_constraint(a, pltpu.HBM)
            for a in (
                filterbank,
                chan_delay.reshape(8, 128),
                tail_len.reshape(1, 128),
                kernels.reshape(64, 256),
                jnp.asarray(block_table()),
            )
        ]
    )
    return power.transpose(1, 0, 2)


def solution(mesh):
    placed = (P("chan", "tm"), P(), P(), P())
    return jax.shard_map(
        shards, mesh=mesh, in_specs=placed, out_specs=P(None, "chan", "tm"), check_vma=False
    )
```

```python
import functools
import math

import jax
import jax.numpy as jnp
import ml_dtypes
import numpy as np
from jax import lax
from jax.experimental import pallas as pl
from jax.experimental.pallas import tpu as pltpu
from jax.sharding import PartitionSpec as P

MESH = pl.DeviceIdType.MESH
NCHAN, NTM, HALF = 32, 8, 16
NEAR_FIRST = list(range(HALF))
F32, BF16 = jnp.float32, jnp.bfloat16

def tables():
    u = np.arange(256)
    m = np.arange(128)
    sums = np.exp(-2j * math.pi * (m[None, :] * u[:, None] % 256) / 256).sum(axis=1) / 16.0
    sums = sums[(u[:, None] + u[None, :]) % 256]
    analytic = np.concatenate([sums.real, sums.imag], axis=1).astype(ml_dtypes.bfloat16)
    angles = 2.0 * math.pi * ((u[:, None] - 128) * u[None, :] % 256) / 256
    taps = np.concatenate([np.cos(angles), np.sin(angles)], axis=1)
    high = taps.astype(ml_dtypes.bfloat16)
    low = (taps - high.astype(np.float64)).astype(ml_dtypes.bfloat16)
    angles = 2.0 * math.pi * (u[:, None] * m[None, :] % 256) / 256
    cosines, sines = np.cos(angles) / 256.0, np.sin(angles) / 256.0
    back = np.concatenate([np.concatenate([cosines, sines], 1), np.concatenate([-sines, cosines], 1)], 0)
    return analytic, np.concatenate([high, low], axis=0), back.astype(ml_dtypes.bfloat16)


def iota(shape, axis):
    return lax.broadcasted_iota(jnp.int32, shape, axis)


def kernel(
    x_hbm, delay_hbm, tail_hbm, taps_hbm, analytic_hbm, split_hbm, back_hbm, out_ref,
    x_ref, delay_ref, tail_ref, taps_ref, analytic_ref, split_ref, back_ref, response, load_sems, xpad, xgroup, acc, stage, send, recv, send_sem, recv_sems, ready_sem, go_sem,
):
    me = lax.axis_index("chan")
    tm = lax.axis_index("tm")
    before, after = lax.rem(tm + NTM - 1, NTM), lax.rem(tm + 1, NTM)

    def other(i):
        return i + (me <= i).astype(jnp.int32)

    pairs = [
        (delay_hbm, delay_ref), (tail_hbm, tail_ref), (x_hbm, x_ref), (taps_hbm, taps_ref),
        (analytic_hbm, analytic_ref), (split_hbm, split_ref), (back_hbm, back_ref),
    ]
    loads = [pltpu.make_async_copy(a, b, load_sems.at[n]) for n, (a, b) in enumerate(pairs)]
    for load in loads[:3]:
        load.start()
    barrier = pltpu.get_barrier_semaphore()

    def tell(sem, p, block):
        pl.semaphore_signal(sem, inc=1, device_id={"chan": p, "tm": block}, device_id_type=MESH)

    first_half, second_half = me < HALF, me >= HALF
    second = me // HALF
    not_first = (tm + NTM - 2) // (NTM - 1)
    last = tm // (NTM - 1)

    @pl.when(first_half)
    def _():
        for p in reversed(range(HALF, NCHAN)):
            tell(barrier, p, tm)

        @pl.when(tm == 1)
        def _():
            tell(barrier, me, 0)

        @pl.when(tm < NTM - 1)
        def _():
            for p in reversed(range(NCHAN)):
                tell(barrier, p, after)

        @pl.when(tm == NTM - 1)
        def _():
            for i in range(HALF - 1):
                tell(barrier, other(i), tm)

    @pl.when(second_half)
    def _():
        for p in range(HALF):
            tell(barrier, p, lax.min(tm + 1, NTM - 1))

    for load in loads[3:]:
        load.start()

    loads[0].wait()
    loads[1].wait()
    row = delay_ref[pl.ds(me // 4, 1), :].astype(F32)
    pick = iota((32, 128), 1) == iota((32, 128), 0) + 32 * lax.rem(me, 4)
    delay = jnp.sum(jnp.where(pick, row, 0.0), axis=1, keepdims=True).astype(jnp.int32)
    tails = jnp.broadcast_to(tail_ref[...], (8, 128))
    lane = iota((8, 128), 1)
    turned = pltpu.roll(tails, 64, 1)
    tails = [jnp.where(lane < 64, tails, turned)[0:1], jnp.where(lane < 64, turned, tails)[0:1]]

    loads[2].wait()
    x = x_ref[...].astype(F32)
    xt = jnp.transpose(jnp.concatenate([x, x, x, x], axis=0))
    xpad[pl.ds(0, 16), :] = jnp.zeros((16, 128), F32)
    xpad[pl.ds(16, 256), :] = xt
    xpad[pl.ds(272, 24), :] = jnp.zeros((24, 128), F32)
    group = iota((288, 128), 1) // 32
    shifted = xpad[pl.ds(0, 288), :]
    for beta in range(1, 4):
        shifted = jnp.where(group == beta, xpad[pl.ds(beta, 288), :], shifted)
    xgroup[...] = shifted
    windows = jnp.concatenate([xgroup[pl.ds(4 * j, 272), :] for j in range(4)], axis=1).astype(BF16)
    sign = (1 - 2 * lax.rem(iota((32, 256), 1), 2)).astype(F32)
    alternating = jnp.sum(x * sign, axis=1, keepdims=True)
    row_sign = (1 - 2 * lax.rem(iota((128, 128), 0), 2)).astype(F32)
    one, zero = jnp.ones((), BF16), jnp.zeros((), BF16)

    def copy_to(kind, p):
        return pltpu.make_async_remote_copy(
            send.at[kind, p], recv.at[kind, me], send_sem, recv_sems.at[kind],
            device_id={"chan": p, "tm": tm if kind else before}, device_id_type=MESH,
        )

    def send_tails(half):
        @pl.when(tm > 0)
        def _():
            for p in range(HALF * half, HALF * half + HALF):
                copy_to(0, p).start()

    def send_bodies(half):
        for i in range(HALF - 1):
            copy_to(1, other(HALF * half + i)).start()

        @pl.when(first_half if half else second_half)
        def _():
            copy_to(1, HALF if half else HALF - 1).start()

    for half in range(2):
        shifts = (delay * tails[half]) >> 12
        shift_bf = (shifts - 16 * (iota((32, 128), 1) // 64)).astype(F32).astype(BF16)

        def one_hot(a):
            return jnp.concatenate(
                [jnp.where(shift_bf == jnp.asarray(32 * a + b, BF16), one, zero) for b in range(16)], axis=0
            )

        acc[...] = jnp.zeros_like(acc)
        for pair in range(4):
            a = 2 * pair
            hot = jnp.concatenate([one_hot(a), one_hot(a + 1)], axis=1)
            part = jnp.dot(windows, hot, preferred_element_type=F32)
            acc[pl.ds(256 - 32 * a, 272), :] += part[:, :128]
            acc[pl.ds(224 - 32 * a, 272), :] += part[:, 128:]
        longest = jnp.where(shift_bf == jnp.asarray(256, BF16), one, zero)
        longest = jnp.concatenate([longest, jnp.zeros((96, 128), BF16)], axis=0)
        acc[pl.ds(0, 272), :] += jnp.dot(windows[:, :128], longest, preferred_element_type=F32)

        parity = (1 - 2 * (shifts & 1)).astype(F32)
        nyquist = jnp.sum(alternating * parity, axis=0, keepdims=True) * (1.0 / 512.0)
        slots = pl.ds(16 * half, 16)
        for q in range(4):
            odd = pltpu.roll(acc[pl.ds(32 + 128 * q, 128), :], 64, 1)
            series = acc[pl.ds(16 + 128 * q, 128), :] + odd - row_sign * nyquist
            if q < 2:
                series = jnp.where(iota((128, 128), 0) + 128 * q >= 256 - tails[half], series, 0.0)
            stage[:, pl.ds(4 * q, 4), :] = jnp.transpose(series)[:64].reshape(16, 4, 128)
        send[0, slots] = stage[:, 0:8, :].astype(BF16)
        send[1, slots] = stage[:, 8:16, :].astype(BF16)
        if half == 0:

            @pl.when(second_half)
            def _():
                pl.semaphore_wait(barrier, HALF + HALF * not_first)

                @pl.when(tm > 0)
                def _():
                    for p in NEAR_FIRST:
                        copy_to(0, p).start()
                        copy_to(1, p).start()

                @pl.when(tm == 0)
                def _():
                    for p in NEAR_FIRST:
                        copy_to(1, p).start()


    @pl.when(first_half)
    def _():
        pl.semaphore_wait(barrier, 1 + (NCHAN - 1) * (not_first + last))

        @pl.when(tm > 0)
        def _():
            tell(ready_sem, me, before)

        send_tails(0)
        send_tails(1)

        @pl.when(tm < NTM - 1)
        def _():
            pl.semaphore_wait(ready_sem, 1)

        tell(go_sem, NCHAN - 4 - me + 2 * lax.rem(me, 4), tm)
        send_bodies(0)
        send_bodies(1)

    @pl.when(second_half)
    def _():
        pl.semaphore_wait(go_sem, 1)
        send_tails(1)
        send_bodies(1)

    for load in loads[3:]:
        load.wait()
    taps = taps_ref[...]
    turned = jnp.dot(taps, split_ref[0:256], preferred_element_type=F32)
    turned += jnp.dot(taps, split_ref[256:512], preferred_element_type=F32)
    response[0] = turned[:32, :256] - turned[32:, 256:]
    response[1] = turned[:32, 256:] + turned[32:, :256]
    recv[1, me] = send[1, me]

    def arrived(kind, count):
        there = recv.at[kind, pl.ds(0, count)]
        return pltpu.make_async_remote_copy(
            there, there, send_sem, recv_sems.at[kind], device_id={"chan": other(0)}, device_id_type=MESH
        )

    tail_all, body_all = arrived(0, NCHAN), arrived(1, NCHAN - 1)
    @pl.when(tm == NTM - 1)
    def _():
        recv[0] = jnp.zeros_like(recv[0])

    body_all.wait_recv()

    @pl.when(tm < NTM - 1)
    def _():
        tail_all.wait_recv()

    total = jnp.sum(recv[0].astype(F32), axis=0) + jnp.sum(recv[1].astype(F32), axis=0)
    series = total * (1.0 / 32.0)
    series = jnp.concatenate([series, pltpu.roll(series, 4, 0)], axis=1).astype(BF16)
    turned = jnp.dot(series, analytic_ref[...], preferred_element_type=F32)
    real, imag = response[0], response[1]
    products = []
    for d in range(4):
        line_real, line_imag = turned[d : d + 1, :256], turned[d : d + 1, 256:]
        products.append(
            jnp.concatenate(
                [real * line_real - imag * line_imag, real * line_imag + imag * line_real], axis=1
            ).astype(BF16)
        )
    corr = jnp.dot(jnp.concatenate(products, axis=0), back_ref[...], preferred_element_type=F32)
    out_ref[...] = (corr[:, :128] * corr[:, :128] + corr[:, 128:] * corr[:, 128:]).astype(BF16).reshape(4, 32, 128)
    body_all.wait_send()

    @pl.when(tm > 0)
    def _():
        tail_all.wait_send()


def shards(filterbank, chan_delay, tail_len, kernels):
    vmem = pl.BlockSpec(memory_space=pltpu.VMEM)
    power = pl.pallas_call(
        kernel,
        out_shape=jax.ShapeDtypeStruct((4, 32, 128), BF16),
        in_specs=[pl.BlockSpec(memory_space=pltpu.HBM)] * 7,
        out_specs=vmem,
        scratch_shapes=[
            pltpu.VMEM((32, 256), BF16),
            pltpu.VMEM((8, 128), jnp.int32),
            pltpu.VMEM((1, 128), jnp.int32),
            pltpu.VMEM((64, 256), BF16),
            pltpu.VMEM((256, 512), BF16),
            pltpu.VMEM((512, 512), BF16),
            pltpu.VMEM((512, 256), BF16),
            pltpu.VMEM((2, 32, 256), F32),
            pltpu.SemaphoreType.DMA((7,)),
            pltpu.VMEM((296, 128), F32),
            pltpu.VMEM((288, 128), F32),
            pltpu.VMEM((544, 128), F32),
            pltpu.VMEM((16, 16, 128), F32),
            pltpu.VMEM((2, NCHAN, 8, 128), BF16),
            pltpu.VMEM((2, NCHAN, 8, 128), BF16),
            pltpu.SemaphoreType.DMA,
            pltpu.SemaphoreType.DMA((2,)),
            pltpu.SemaphoreType.REGULAR,
            pltpu.SemaphoreType.REGULAR,
        ],
        compiler_params=pltpu.CompilerParams(
            collective_id=0, has_side_effects=True, vmem_limit_bytes=32 * 1024 * 1024
        ),
        name="dedisperse",
    )(
        *[
            pltpu.with_memory_space_constraint(a, pltpu.HBM)
            for a in (
                filterbank,
                chan_delay.reshape(8, 128),
                tail_len.reshape(1, 128),
                kernels.reshape(64, 256),
                *map(jnp.asarray, tables()),
            )
        ]
    )
    return power.transpose(1, 0, 2)


def solution(mesh):
    placed = (P("chan", "tm"), P(), P(), P())
    return jax.shard_map(
        shards, mesh=mesh, in_specs=placed, out_specs=P(None, "chan", "tm"), check_vma=False
    )
```

```python
import functools
import math

import jax
import jax.numpy as jnp
import ml_dtypes
import numpy as np
from jax import lax
from jax.experimental import pallas as pl
from jax.experimental.pallas import tpu as pltpu
from jax.sharding import PartitionSpec as P

MESH = pl.DeviceIdType.MESH
NCHAN, NTM, HALF = 32, 8, 16
F32, BF16 = jnp.float32, jnp.bfloat16

def tables():
    u = np.arange(256)
    m = np.arange(128)
    sums = np.exp(-2j * math.pi * (m[None, :] * u[:, None] % 256) / 256).sum(axis=1) / 16.0
    sums = sums[(u[:, None] + u[None, :]) % 256]
    analytic = np.concatenate([sums.real, sums.imag], axis=1).astype(ml_dtypes.bfloat16)
    angles = 2.0 * math.pi * ((u[:, None] - 128) * u[None, :] % 256) / 256
    taps = np.concatenate([np.cos(angles), np.sin(angles)], axis=1)
    high = taps.astype(ml_dtypes.bfloat16)
    low = (taps - high.astype(np.float64)).astype(ml_dtypes.bfloat16)
    angles = 2.0 * math.pi * (u[:, None] * m[None, :] % 256) / 256
    cosines, sines = np.cos(angles) / 256.0, np.sin(angles) / 256.0
    back = np.concatenate([np.concatenate([cosines, sines], 1), np.concatenate([-sines, cosines], 1)], 0)
    return analytic, np.concatenate([high, low], axis=0), back.astype(ml_dtypes.bfloat16)


def iota(shape, axis):
    return lax.broadcasted_iota(jnp.int32, shape, axis)


def kernel(
    x_hbm, delay_hbm, tail_hbm, taps_hbm, analytic_hbm, split_hbm, back_hbm, out_ref,
    x_ref, delay_ref, tail_ref, taps_ref, analytic_ref, split_ref, back_ref, response, load_sems, xpad, xgroup, acc, stage, send, recv, send_sem, recv_sems, ready_sem, go_sem,
):
    me = lax.axis_index("chan")
    tm = lax.axis_index("tm")
    before, after = lax.rem(tm + NTM - 1, NTM), lax.rem(tm + 1, NTM)

    def other(i):
        return i + (me <= i).astype(jnp.int32)

    pairs = [
        (delay_hbm, delay_ref), (tail_hbm, tail_ref), (x_hbm, x_ref), (taps_hbm, taps_ref),
        (analytic_hbm, analytic_ref), (split_hbm, split_ref), (back_hbm, back_ref),
    ]
    loads = [pltpu.make_async_copy(a, b, load_sems.at[n]) for n, (a, b) in enumerate(pairs)]
    for load in loads[:3]:
        load.start()
    barrier = pltpu.get_barrier_semaphore()

    def tell(sem, p, block):
        pl.semaphore_signal(sem, inc=1, device_id={"chan": p, "tm": block}, device_id_type=MESH)

    first_half, second_half = me < HALF, me >= HALF
    second = me // HALF
    not_first = (tm + NTM - 2) // (NTM - 1)
    last = tm // (NTM - 1)

    @pl.when(tm == 1)
    def _():
        tell(barrier, me, 0)

    @pl.when(first_half)
    def _():
        @pl.when(tm < NTM - 1)
        def _():
            for p in reversed(range(NCHAN)):
                tell(barrier, p, after)

        @pl.when(tm == NTM - 1)
        def _():
            for p in reversed(range(HALF, NCHAN)):
                tell(barrier, p, tm)
            for i in range(HALF - 1):
                tell(barrier, other(i), tm)

    @pl.when(second_half)
    def _():
        @pl.when(tm < NTM - 1)
        def _():
            tell(barrier, me, after)

        for p in range(HALF):
            tell(barrier, p, lax.min(tm + 1, NTM - 1))

    for load in loads[3:]:
        load.start()

    loads[0].wait()
    loads[1].wait()
    row = delay_ref[pl.ds(me // 4, 1), :].astype(F32)
    pick = iota((32, 128), 1) == iota((32, 128), 0) + 32 * lax.rem(me, 4)
    delay = jnp.sum(jnp.where(pick, row, 0.0), axis=1, keepdims=True).astype(jnp.int32)
    tails = jnp.broadcast_to(tail_ref[...], (8, 128))
    lane = iota((8, 128), 1)
    turned = pltpu.roll(tails, 64, 1)
    tails = [jnp.where(lane < 64, tails, turned)[0:1], jnp.where(lane < 64, turned, tails)[0:1]]

    loads[2].wait()
    x = x_ref[...].astype(F32)
    xt = jnp.transpose(jnp.concatenate([x, x, x, x], axis=0))
    xpad[pl.ds(0, 16), :] = jnp.zeros((16, 128), F32)
    xpad[pl.ds(16, 256), :] = xt
    xpad[pl.ds(272, 24), :] = jnp.zeros((24, 128), F32)
    group = iota((288, 128), 1) // 32
    shifted = xpad[pl.ds(0, 288), :]
    for beta in range(1, 4):
        shifted = jnp.where(group == beta, xpad[pl.ds(beta, 288), :], shifted)
    xgroup[...] = shifted
    windows = jnp.concatenate([xgroup[pl.ds(4 * j, 272), :] for j in range(4)], axis=1).astype(BF16)
    sign = (1 - 2 * lax.rem(iota((32, 256), 1), 2)).astype(F32)
    alternating = jnp.sum(x * sign, axis=1, keepdims=True)
    row_sign = (1 - 2 * lax.rem(iota((128, 128), 0), 2)).astype(F32)
    one, zero = jnp.ones((), BF16), jnp.zeros((), BF16)

    def copy_to(kind, p):
        return pltpu.make_async_remote_copy(
            send.at[kind, p], recv.at[kind, me], send_sem, recv_sems.at[kind],
            device_id={"chan": p, "tm": tm if kind else before}, device_id_type=MESH,
        )

    def send_tails(half):
        @pl.when(tm > 0)
        def _():
            for p in range(HALF * half, HALF * half + HALF):
                copy_to(0, p).start()

    def send_bodies(half):
        for i in range(HALF - 1):
            copy_to(1, other(HALF * half + i)).start()

        @pl.when(first_half if half else second_half)
        def _():
            copy_to(1, HALF if half else HALF - 1).start()

    for half in range(2):
        shifts = (delay * tails[half]) >> 12
        shift_bf = (shifts - 16 * (iota((32, 128), 1) // 64)).astype(F32).astype(BF16)

        def one_hot(a):
            return jnp.concatenate(
                [jnp.where(shift_bf == jnp.asarray(32 * a + b, BF16), one, zero) for b in range(16)], axis=0
            )

        acc[...] = jnp.zeros_like(acc)
        for pair in range(4):
            a = 2 * pair
            hot = jnp.concatenate([one_hot(a), one_hot(a + 1)], axis=1)
            part = jnp.dot(windows, hot, preferred_element_type=F32)
            acc[pl.ds(256 - 32 * a, 272), :] += part[:, :128]
            acc[pl.ds(224 - 32 * a, 272), :] += part[:, 128:]
        longest = jnp.where(shift_bf == jnp.asarray(256, BF16), one, zero)
        longest = jnp.concatenate([longest, jnp.zeros((96, 128), BF16)], axis=0)
        acc[pl.ds(0, 272), :] += jnp.dot(windows[:, :128], longest, preferred_element_type=F32)

        parity = (1 - 2 * (shifts & 1)).astype(F32)
        nyquist = jnp.sum(alternating * parity, axis=0, keepdims=True) * (1.0 / 512.0)
        slots = pl.ds(16 * half, 16)
        for q in range(4):
            odd = pltpu.roll(acc[pl.ds(32 + 128 * q, 128), :], 64, 1)
            series = acc[pl.ds(16 + 128 * q, 128), :] + odd - row_sign * nyquist
            if q < 2:
                series = jnp.where(iota((128, 128), 0) + 128 * q >= 256 - tails[half], series, 0.0)
            stage[:, pl.ds(4 * q, 4), :] = jnp.transpose(series)[:64].reshape(16, 4, 128)
        send[0, slots] = stage[:, 0:8, :].astype(BF16)
        send[1, slots] = stage[:, 8:16, :].astype(BF16)
        if half == 0:

            @pl.when(second_half)
            def _():
                pl.semaphore_wait(barrier, 1 + HALF * (not_first + last))

                @pl.when(tm > 0)
                def _():
                    tell(ready_sem, me, before)

                send_tails(0)

                @pl.when(tm < NTM - 1)
                def _():
                    pl.semaphore_wait(ready_sem, 1)

                send_bodies(0)

    @pl.when(first_half)
    def _():
        pl.semaphore_wait(barrier, 1 + (NCHAN - 1) * (not_first + last))

        @pl.when(tm > 0)
        def _():
            tell(ready_sem, me, before)

        send_tails(0)
        send_tails(1)

        @pl.when(tm < NTM - 1)
        def _():
            pl.semaphore_wait(ready_sem, 1)

        tell(go_sem, NCHAN - 4 - me + 2 * lax.rem(me, 4), tm)
        send_bodies(0)
        send_bodies(1)

    @pl.when(second_half)
    def _():
        pl.semaphore_wait(go_sem, 1)
        send_tails(1)
        send_bodies(1)

    for load in loads[3:]:
        load.wait()
    taps = taps_ref[...]
    turned = jnp.dot(taps, split_ref[0:256], preferred_element_type=F32)
    turned += jnp.dot(taps, split_ref[256:512], preferred_element_type=F32)
    response[0] = turned[:32, :256] - turned[32:, 256:]
    response[1] = turned[:32, 256:] + turned[32:, :256]
    recv[1, me] = send[1, me]

    def arrived(kind, count):
        there = recv.at[kind, pl.ds(0, count)]
        return pltpu.make_async_remote_copy(
            there, there, send_sem, recv_sems.at[kind], device_id={"chan": other(0)}, device_id_type=MESH
        )

    tail_all, body_all = arrived(0, NCHAN), arrived(1, NCHAN - 1)
    @pl.when(tm == NTM - 1)
    def _():
        recv[0] = jnp.zeros_like(recv[0])

    body_all.wait_recv()

    @pl.when(tm < NTM - 1)
    def _():
        tail_all.wait_recv()

    total = jnp.sum(recv[0].astype(F32), axis=0) + jnp.sum(recv[1].astype(F32), axis=0)
    series = total * (1.0 / 32.0)
    series = jnp.concatenate([series, pltpu.roll(series, 4, 0)], axis=1).astype(BF16)
    turned = jnp.dot(series, analytic_ref[...], preferred_element_type=F32)
    real, imag = response[0], response[1]
    products = []
    for d in range(4):
        line_real, line_imag = turned[d : d + 1, :256], turned[d : d + 1, 256:]
        products.append(
            jnp.concatenate(
                [real * line_real - imag * line_imag, real * line_imag + imag * line_real], axis=1
            ).astype(BF16)
        )
    corr = jnp.dot(jnp.concatenate(products, axis=0), back_ref[...], preferred_element_type=F32)
    out_ref[...] = (corr[:, :128] * corr[:, :128] + corr[:, 128:] * corr[:, 128:]).astype(BF16).reshape(4, 32, 128)
    body_all.wait_send()

    @pl.when(tm > 0)
    def _():
        tail_all.wait_send()


def shards(filterbank, chan_delay, tail_len, kernels):
    vmem = pl.BlockSpec(memory_space=pltpu.VMEM)
    power = pl.pallas_call(
        kernel,
        out_shape=jax.ShapeDtypeStruct((4, 32, 128), BF16),
        in_specs=[pl.BlockSpec(memory_space=pltpu.HBM)] * 7,
        out_specs=vmem,
        scratch_shapes=[
            pltpu.VMEM((32, 256), BF16),
            pltpu.VMEM((8, 128), jnp.int32),
            pltpu.VMEM((1, 128), jnp.int32),
            pltpu.VMEM((64, 256), BF16),
            pltpu.VMEM((256, 512), BF16),
            pltpu.VMEM((512, 512), BF16),
            pltpu.VMEM((512, 256), BF16),
            pltpu.VMEM((2, 32, 256), F32),
            pltpu.SemaphoreType.DMA((7,)),
            pltpu.VMEM((296, 128), F32),
            pltpu.VMEM((288, 128), F32),
            pltpu.VMEM((544, 128), F32),
            pltpu.VMEM((16, 16, 128), F32),
            pltpu.VMEM((2, NCHAN, 8, 128), BF16),
            pltpu.VMEM((2, NCHAN, 8, 128), BF16),
            pltpu.SemaphoreType.DMA,
            pltpu.SemaphoreType.DMA((2,)),
            pltpu.SemaphoreType.REGULAR,
            pltpu.SemaphoreType.REGULAR,
        ],
        compiler_params=pltpu.CompilerParams(
            collective_id=0, has_side_effects=True, vmem_limit_bytes=32 * 1024 * 1024
        ),
        name="dedisperse",
    )(
        *[
            pltpu.with_memory_space_constraint(a, pltpu.HBM)
            for a in (
                filterbank,
                chan_delay.reshape(8, 128),
                tail_len.reshape(1, 128),
                kernels.reshape(64, 256),
                *map(jnp.asarray, tables()),
            )
        ]
    )
    return power.transpose(1, 0, 2)


def solution(mesh):
    placed = (P("chan", "tm"), P(), P(), P())
    return jax.shard_map(
        shards, mesh=mesh, in_specs=placed, out_specs=P(None, "chan", "tm"), check_vma=False
    )
```

```python
import functools
import math

import jax
import jax.numpy as jnp
import ml_dtypes
import numpy as np
from jax import lax
from jax.experimental import pallas as pl
from jax.experimental.pallas import tpu as pltpu
from jax.sharding import PartitionSpec as P

MESH = pl.DeviceIdType.MESH
NCHAN, NTM, HALF = 32, 8, 16
F32, BF16 = jnp.float32, jnp.bfloat16

def tables():
    u = np.arange(256)
    m = np.arange(128)
    sums = np.exp(-2j * math.pi * (m[None, :] * u[:, None] % 256) / 256).sum(axis=1) / 16.0
    sums = sums[(u[:, None] + u[None, :]) % 256]
    analytic = np.concatenate([sums.real, sums.imag], axis=1).astype(ml_dtypes.bfloat16)
    angles = 2.0 * math.pi * ((u[:, None] - 128) * u[None, :] % 256) / 256
    taps = np.concatenate([np.cos(angles), np.sin(angles)], axis=1)
    high = taps.astype(ml_dtypes.bfloat16)
    low = (taps - high.astype(np.float64)).astype(ml_dtypes.bfloat16)
    angles = 2.0 * math.pi * (u[:, None] * m[None, :] % 256) / 256
    cosines, sines = np.cos(angles) / 256.0, np.sin(angles) / 256.0
    back = np.concatenate([np.concatenate([cosines, sines], 1), np.concatenate([-sines, cosines], 1)], 0)
    return analytic, np.concatenate([high, low], axis=0), back.astype(ml_dtypes.bfloat16)


def iota(shape, axis):
    return lax.broadcasted_iota(jnp.int32, shape, axis)


def kernel(
    x_hbm, delay_hbm, tail_hbm, taps_hbm, analytic_hbm, split_hbm, back_hbm, out_ref,
    x_ref, delay_ref, tail_ref, taps_ref, analytic_ref, split_ref, back_ref, response, load_sems, xpad, xgroup, acc, stage, send, recv, send_sem, recv_sems, ready_sem, go_sem,
):
    me = lax.axis_index("chan")
    tm = lax.axis_index("tm")
    before, after = lax.rem(tm + NTM - 1, NTM), lax.rem(tm + 1, NTM)

    def other(i):
        return i + (me <= i).astype(jnp.int32)

    pairs = [
        (delay_hbm, delay_ref), (tail_hbm, tail_ref), (x_hbm, x_ref), (taps_hbm, taps_ref),
        (analytic_hbm, analytic_ref), (split_hbm, split_ref), (back_hbm, back_ref),
    ]
    loads = [pltpu.make_async_copy(a, b, load_sems.at[n]) for n, (a, b) in enumerate(pairs)]
    barrier = pltpu.get_barrier_semaphore()

    def tell(sem, p, block):
        pl.semaphore_signal(sem, inc=1, device_id={"chan": p, "tm": block}, device_id_type=MESH)

    first_half, second_half = me < HALF, me >= HALF
    second = me // HALF
    not_first = (tm + NTM - 2) // (NTM - 1)
    last = tm // (NTM - 1)

    @pl.when(tm == 1)
    def _():
        tell(barrier, me, 0)

    @pl.when(first_half)
    def _():
        @pl.when(tm < NTM - 1)
        def _():
            for p in reversed(range(NCHAN)):
                tell(barrier, p, after)

        @pl.when(tm == NTM - 1)
        def _():
            for p in reversed(range(HALF, NCHAN)):
                tell(barrier, p, tm)
            for i in range(HALF - 1):
                tell(barrier, other(i), tm)

    @pl.when(second_half)
    def _():
        for p in range(HALF):
            tell(barrier, p, lax.min(tm + 1, NTM - 1))

        @pl.when(tm < NTM - 1)
        def _():
            tell(barrier, me, after)

    for load in loads:
        load.start()

    loads[0].wait()
    loads[1].wait()
    row = delay_ref[pl.ds(me // 4, 1), :].astype(F32)
    pick = iota((32, 128), 1) == iota((32, 128), 0) + 32 * lax.rem(me, 4)
    delay = jnp.sum(jnp.where(pick, row, 0.0), axis=1, keepdims=True).astype(jnp.int32)
    tails = jnp.broadcast_to(tail_ref[...], (8, 128))
    lane = iota((8, 128), 1)
    turned = pltpu.roll(tails, 64, 1)
    tails = [jnp.where(lane < 64, tails, turned)[0:1], jnp.where(lane < 64, turned, tails)[0:1]]

    loads[2].wait()
    x = x_ref[...].astype(F32)
    xt = jnp.transpose(jnp.concatenate([x, x, x, x], axis=0))
    xpad[pl.ds(0, 16), :] = jnp.zeros((16, 128), F32)
    xpad[pl.ds(16, 256), :] = xt
    xpad[pl.ds(272, 24), :] = jnp.zeros((24, 128), F32)
    group = iota((288, 128), 1) // 32
    shifted = xpad[pl.ds(0, 288), :]
    for beta in range(1, 4):
        shifted = jnp.where(group == beta, xpad[pl.ds(beta, 288), :], shifted)
    xgroup[...] = shifted
    windows = jnp.concatenate([xgroup[pl.ds(4 * j, 272), :] for j in range(4)], axis=1).astype(BF16)
    sign = (1 - 2 * lax.rem(iota((32, 256), 1), 2)).astype(F32)
    alternating = jnp.sum(x * sign, axis=1, keepdims=True)
    row_sign = (1 - 2 * lax.rem(iota((128, 128), 0), 2)).astype(F32)
    one, zero = jnp.ones((), BF16), jnp.zeros((), BF16)

    def copy_to(kind, p):
        return pltpu.make_async_remote_copy(
            send.at[kind, p], recv.at[kind, me], send_sem, recv_sems.at[kind],
            device_id={"chan": p, "tm": tm if kind else before}, device_id_type=MESH,
        )

    def send_tails(half):
        @pl.when(tm > 0)
        def _():
            for p in range(HALF * half, HALF * half + HALF):
                copy_to(0, p).start()

    def send_bodies(half):
        for i in range(HALF - 1):
            copy_to(1, other(HALF * half + i)).start()

        @pl.when(first_half if half else second_half)
        def _():
            copy_to(1, HALF if half else HALF - 1).start()

    for half in range(2):
        shifts = (delay * tails[half]) >> 12
        shift_bf = (shifts - 16 * (iota((32, 128), 1) // 64)).astype(F32).astype(BF16)

        def one_hot(a):
            return jnp.concatenate(
                [jnp.where(shift_bf == jnp.asarray(32 * a + b, BF16), one, zero) for b in range(16)], axis=0
            )

        acc[...] = jnp.zeros_like(acc)
        for pair in range(4):
            a = 2 * pair
            hot = jnp.concatenate([one_hot(a), one_hot(a + 1)], axis=1)
            part = jnp.dot(windows, hot, preferred_element_type=F32)
            acc[pl.ds(256 - 32 * a, 272), :] += part[:, :128]
            acc[pl.ds(224 - 32 * a, 272), :] += part[:, 128:]
        longest = jnp.where(shift_bf == jnp.asarray(256, BF16), one, zero)
        longest = jnp.concatenate([longest, jnp.zeros((96, 128), BF16)], axis=0)
        acc[pl.ds(0, 272), :] += jnp.dot(windows[:, :128], longest, preferred_element_type=F32)

        parity = (1 - 2 * (shifts & 1)).astype(F32)
        nyquist = jnp.sum(alternating * parity, axis=0, keepdims=True) * (1.0 / 512.0)
        slots = pl.ds(16 * half, 16)
        for q in range(4):
            odd = pltpu.roll(acc[pl.ds(32 + 128 * q, 128), :], 64, 1)
            series = acc[pl.ds(16 + 128 * q, 128), :] + odd - row_sign * nyquist
            if q < 2:
                series = jnp.where(iota((128, 128), 0) + 128 * q >= 256 - tails[half], series, 0.0)
            stage[:, pl.ds(4 * q, 4), :] = jnp.transpose(series)[:64].reshape(16, 4, 128)
        send[0, slots] = stage[:, 0:8, :].astype(BF16)
        send[1, slots] = stage[:, 8:16, :].astype(BF16)
        if half == 0:

            @pl.when(second_half)
            def _():
                pl.semaphore_wait(barrier, 1 + HALF * (not_first + last))

                @pl.when(tm > 0)
                def _():
                    tell(ready_sem, me, before)

                send_tails(0)

                @pl.when(tm < NTM - 1)
                def _():
                    pl.semaphore_wait(ready_sem, 1)

                send_bodies(0)

    @pl.when(first_half)
    def _():
        pl.semaphore_wait(barrier, 1 + (NCHAN - 1) * (not_first + last))

        @pl.when(tm > 0)
        def _():
            tell(ready_sem, me, before)

        send_tails(0)

        @pl.when(tm < NTM - 1)
        def _():
            pl.semaphore_wait(ready_sem, 1)

        tell(go_sem, NCHAN - 4 - me + 2 * lax.rem(me, 4), tm)
        send_bodies(0)
        send_tails(1)
        send_bodies(1)

    @pl.when(second_half)
    def _():
        pl.semaphore_wait(go_sem, 1)
        send_tails(1)
        send_bodies(1)

    for load in loads[3:]:
        load.wait()
    taps = taps_ref[...]
    turned = jnp.dot(taps, split_ref[0:256], preferred_element_type=F32)
    turned += jnp.dot(taps, split_ref[256:512], preferred_element_type=F32)
    response[0] = turned[:32, :256] - turned[32:, 256:]
    response[1] = turned[:32, 256:] + turned[32:, :256]
    recv[1, me] = send[1, me]

    def arrived(kind, count):
        there = recv.at[kind, pl.ds(0, count)]
        return pltpu.make_async_remote_copy(
            there, there, send_sem, recv_sems.at[kind], device_id={"chan": other(0)}, device_id_type=MESH
        )

    tail_all, body_all = arrived(0, NCHAN), arrived(1, NCHAN - 1)
    @pl.when(tm == NTM - 1)
    def _():
        recv[0] = jnp.zeros_like(recv[0])

    body_all.wait_recv()

    @pl.when(tm < NTM - 1)
    def _():
        tail_all.wait_recv()

    total = jnp.sum(recv[0].astype(F32), axis=0) + jnp.sum(recv[1].astype(F32), axis=0)
    series = total * (1.0 / 32.0)
    series = jnp.concatenate([series, pltpu.roll(series, 4, 0)], axis=1).astype(BF16)
    turned = jnp.dot(series, analytic_ref[...], preferred_element_type=F32)
    real, imag = response[0], response[1]
    products = []
    for d in range(4):
        line_real, line_imag = turned[d : d + 1, :256], turned[d : d + 1, 256:]
        products.append(
            jnp.concatenate(
                [real * line_real - imag * line_imag, real * line_imag + imag * line_real], axis=1
            ).astype(BF16)
        )
    corr = jnp.dot(jnp.concatenate(products, axis=0), back_ref[...], preferred_element_type=F32)
    out_ref[...] = (corr[:, :128] * corr[:, :128] + corr[:, 128:] * corr[:, 128:]).astype(BF16).reshape(4, 32, 128)
    body_all.wait_send()

    @pl.when(tm > 0)
    def _():
        tail_all.wait_send()


def shards(filterbank, chan_delay, tail_len, kernels):
    vmem = pl.BlockSpec(memory_space=pltpu.VMEM)
    power = pl.pallas_call(
        kernel,
        out_shape=jax.ShapeDtypeStruct((4, 32, 128), BF16),
        in_specs=[pl.BlockSpec(memory_space=pltpu.HBM)] * 7,
        out_specs=vmem,
        scratch_shapes=[
            pltpu.VMEM((32, 256), BF16),
            pltpu.VMEM((8, 128), jnp.int32),
            pltpu.VMEM((1, 128), jnp.int32),
            pltpu.VMEM((64, 256), BF16),
            pltpu.VMEM((256, 512), BF16),
            pltpu.VMEM((512, 512), BF16),
            pltpu.VMEM((512, 256), BF16),
            pltpu.VMEM((2, 32, 256), F32),
            pltpu.SemaphoreType.DMA((7,)),
            pltpu.VMEM((296, 128), F32),
            pltpu.VMEM((288, 128), F32),
            pltpu.VMEM((544, 128), F32),
            pltpu.VMEM((16, 16, 128), F32),
            pltpu.VMEM((2, NCHAN, 8, 128), BF16),
            pltpu.VMEM((2, NCHAN, 8, 128), BF16),
            pltpu.SemaphoreType.DMA,
            pltpu.SemaphoreType.DMA((2,)),
            pltpu.SemaphoreType.REGULAR,
            pltpu.SemaphoreType.REGULAR,
        ],
        compiler_params=pltpu.CompilerParams(
            collective_id=0, has_side_effects=True, vmem_limit_bytes=32 * 1024 * 1024
        ),
        name="dedisperse",
    )(
        *[
            pltpu.with_memory_space_constraint(a, pltpu.HBM)
            for a in (
                filterbank,
                chan_delay.reshape(8, 128),
                tail_len.reshape(1, 128),
                kernels.reshape(64, 256),
                *map(jnp.asarray, tables()),
            )
        ]
    )
    return power.transpose(1, 0, 2)


def solution(mesh):
    placed = (P("chan", "tm"), P(), P(), P())
    return jax.shard_map(
        shards, mesh=mesh, in_specs=placed, out_specs=P(None, "chan", "tm"), check_vma=False
    )
```

```python
import functools
import math

import jax
import jax.numpy as jnp
import ml_dtypes
import numpy as np
from jax import lax
from jax.experimental import pallas as pl
from jax.experimental.pallas import tpu as pltpu
from jax.sharding import PartitionSpec as P

MESH = pl.DeviceIdType.MESH
NCHAN, NTM, HALF = 32, 8, 16
F32, BF16 = jnp.float32, jnp.bfloat16

def tables():
    u = np.arange(256)
    m = np.arange(128)
    sums = np.exp(-2j * math.pi * (m[None, :] * u[:, None] % 256) / 256).sum(axis=1) / 16.0
    sums = sums[(u[:, None] + u[None, :]) % 256]
    analytic = np.concatenate([sums.real, sums.imag], axis=1).astype(ml_dtypes.bfloat16)
    angles = 2.0 * math.pi * ((u[:, None] - 128) * u[None, :] % 256) / 256
    taps = np.concatenate([np.cos(angles), np.sin(angles)], axis=1)
    high = taps.astype(ml_dtypes.bfloat16)
    low = (taps - high.astype(np.float64)).astype(ml_dtypes.bfloat16)
    angles = 2.0 * math.pi * (u[:, None] * m[None, :] % 256) / 256
    cosines, sines = np.cos(angles) / 256.0, np.sin(angles) / 256.0
    back = np.concatenate([np.concatenate([cosines, sines], 1), np.concatenate([-sines, cosines], 1)], 0)
    return analytic, np.concatenate([high, low], axis=0), back.astype(ml_dtypes.bfloat16)


def iota(shape, axis):
    return lax.broadcasted_iota(jnp.int32, shape, axis)


def kernel(
    x_hbm, delay_hbm, tail_hbm, taps_hbm, analytic_hbm, split_hbm, back_hbm, out_ref,
    x_ref, delay_ref, tail_ref, taps_ref, analytic_ref, split_ref, back_ref, response, load_sems, xpad, xgroup, acc, stage, send, recv, send_sem, recv_sems, ready_sem, go_sem, all_sem,
):
    me = lax.axis_index("chan")
    tm = lax.axis_index("tm")
    before, after = lax.rem(tm + NTM - 1, NTM), lax.rem(tm + 1, NTM)

    def other(i):
        return i + (me <= i).astype(jnp.int32)

    pairs = [
        (delay_hbm, delay_ref), (tail_hbm, tail_ref), (x_hbm, x_ref), (taps_hbm, taps_ref),
        (analytic_hbm, analytic_ref), (split_hbm, split_ref), (back_hbm, back_ref),
    ]
    loads = [pltpu.make_async_copy(a, b, load_sems.at[n]) for n, (a, b) in enumerate(pairs)]
    barrier = pltpu.get_barrier_semaphore()

    def tell(sem, p, block):
        pl.semaphore_signal(sem, inc=1, device_id={"chan": p, "tm": block}, device_id_type=MESH)

    first_half, second_half = me < HALF, me >= HALF
    mirror = NCHAN - 4 - me + 2 * lax.rem(me, 4)
    not_first = (tm + NTM - 2) // (NTM - 1)
    last = tm // (NTM - 1)

    @pl.when(tm == 1)
    def _():
        tell(barrier, me, 0)

    @pl.when(first_half)
    def _():
        @pl.when(tm < NTM - 1)
        def _():
            for p in reversed(range(NCHAN)):
                tell(barrier, p, after)

        @pl.when(tm == NTM - 1)
        def _():
            for p in reversed(range(HALF, NCHAN)):
                tell(barrier, p, tm)
            for i in range(HALF - 1):
                tell(barrier, other(i), tm)

    @pl.when(second_half)
    def _():
        for p in range(HALF):
            tell(barrier, p, lax.min(tm + 1, NTM - 1))

        @pl.when(tm < NTM - 1)
        def _():
            tell(barrier, me, after)

    for load in loads:
        load.start()

    loads[0].wait()
    loads[1].wait()
    row = delay_ref[pl.ds(me // 4, 1), :].astype(F32)
    pick = iota((32, 128), 1) == iota((32, 128), 0) + 32 * lax.rem(me, 4)
    delay = jnp.sum(jnp.where(pick, row, 0.0), axis=1, keepdims=True).astype(jnp.int32)
    tails = jnp.broadcast_to(tail_ref[...], (8, 128))
    lane = iota((8, 128), 1)
    turned = pltpu.roll(tails, 64, 1)
    tails = [jnp.where(lane < 64, tails, turned)[0:1], jnp.where(lane < 64, turned, tails)[0:1]]

    loads[2].wait()
    x = x_ref[...].astype(F32)
    xt = jnp.transpose(jnp.concatenate([x, x, x, x], axis=0))
    xpad[pl.ds(0, 16), :] = jnp.zeros((16, 128), F32)
    xpad[pl.ds(16, 256), :] = xt
    xpad[pl.ds(272, 24), :] = jnp.zeros((24, 128), F32)
    group = iota((288, 128), 1) // 32
    shifted = xpad[pl.ds(0, 288), :]
    for beta in range(1, 4):
        shifted = jnp.where(group == beta, xpad[pl.ds(beta, 288), :], shifted)
    xgroup[...] = shifted
    windows = jnp.concatenate([xgroup[pl.ds(4 * j, 272), :] for j in range(4)], axis=1).astype(BF16)
    sign = (1 - 2 * lax.rem(iota((32, 256), 1), 2)).astype(F32)
    alternating = jnp.sum(x * sign, axis=1, keepdims=True)
    row_sign = (1 - 2 * lax.rem(iota((128, 128), 0), 2)).astype(F32)
    one, zero = jnp.ones((), BF16), jnp.zeros((), BF16)

    def copy_to(kind, p):
        return pltpu.make_async_remote_copy(
            send.at[kind, p], recv.at[kind, me], send_sem, recv_sems.at[kind],
            device_id={"chan": p, "tm": tm if kind else before}, device_id_type=MESH,
        )

    def send_tails(half):
        @pl.when(tm > 0)
        def _():
            for p in range(HALF * half, HALF * half + HALF):
                copy_to(0, p).start()

    def send_bodies(half):
        for i in range(HALF - 1):
            copy_to(1, other(HALF * half + i)).start()

        @pl.when(first_half if half else second_half)
        def _():
            copy_to(1, HALF if half else HALF - 1).start()

    for half in range(2):
        shifts = (delay * tails[half]) >> 12
        shift_bf = (shifts - 16 * (iota((32, 128), 1) // 64)).astype(F32).astype(BF16)

        def one_hot(a):
            return jnp.concatenate(
                [jnp.where(shift_bf == jnp.asarray(32 * a + b, BF16), one, zero) for b in range(16)], axis=0
            )

        acc[...] = jnp.zeros_like(acc)
        for pair in range(4):
            a = 2 * pair
            hot = jnp.concatenate([one_hot(a), one_hot(a + 1)], axis=1)
            part = jnp.dot(windows, hot, preferred_element_type=F32)
            acc[pl.ds(256 - 32 * a, 272), :] += part[:, :128]
            acc[pl.ds(224 - 32 * a, 272), :] += part[:, 128:]
        longest = jnp.where(shift_bf == jnp.asarray(256, BF16), one, zero)
        longest = jnp.concatenate([longest, jnp.zeros((96, 128), BF16)], axis=0)
        acc[pl.ds(0, 272), :] += jnp.dot(windows[:, :128], longest, preferred_element_type=F32)

        parity = (1 - 2 * (shifts & 1)).astype(F32)
        nyquist = jnp.sum(alternating * parity, axis=0, keepdims=True) * (1.0 / 512.0)
        slots = pl.ds(16 * half, 16)
        for q in range(4):
            odd = pltpu.roll(acc[pl.ds(32 + 128 * q, 128), :], 64, 1)
            series = acc[pl.ds(16 + 128 * q, 128), :] + odd - row_sign * nyquist
            if q < 2:
                series = jnp.where(iota((128, 128), 0) + 128 * q >= 256 - tails[half], series, 0.0)
            stage[:, pl.ds(4 * q, 4), :] = jnp.transpose(series)[:64].reshape(16, 4, 128)
        send[0, slots] = stage[:, 0:8, :].astype(BF16)
        send[1, slots] = stage[:, 8:16, :].astype(BF16)
        if half == 0:

            @pl.when(second_half)
            def _():
                pl.semaphore_wait(barrier, 1 + HALF * (not_first + last))

                @pl.when(tm > 0)
                def _():
                    tell(ready_sem, mirror, before)
                    tell(ready_sem, me, before)

                send_tails(0)

                @pl.when(tm < NTM - 1)
                def _():
                    pl.semaphore_wait(ready_sem, 1)

                send_bodies(0)

    @pl.when(first_half)
    def _():
        pl.semaphore_wait(barrier, 1 + (NCHAN - 1) * (not_first + last))

        @pl.when(tm > 0)
        def _():
            tell(all_sem, me, before)

        send_tails(0)

        @pl.when(tm < NTM - 1)
        def _():
            pl.semaphore_wait(ready_sem, 1)

        send_bodies(0)
        send_tails(1)

        @pl.when(tm < NTM - 1)
        def _():
            pl.semaphore_wait(all_sem, 1)

        tell(go_sem, mirror, tm)
        send_bodies(1)

    @pl.when(second_half)
    def _():
        pl.semaphore_wait(go_sem, 1)
        send_tails(1)
        send_bodies(1)

    for load in loads[3:]:
        load.wait()
    taps = taps_ref[...]
    turned = jnp.dot(taps, split_ref[0:256], preferred_element_type=F32)
    turned += jnp.dot(taps, split_ref[256:512], preferred_element_type=F32)
    response[0] = turned[:32, :256] - turned[32:, 256:]
    response[1] = turned[:32, 256:] + turned[32:, :256]
    recv[1, me] = send[1, me]

    def arrived(kind, count):
        there = recv.at[kind, pl.ds(0, count)]
        return pltpu.make_async_remote_copy(
            there, there, send_sem, recv_sems.at[kind], device_id={"chan": other(0)}, device_id_type=MESH
        )

    tail_all, body_all = arrived(0, NCHAN), arrived(1, NCHAN - 1)
    @pl.when(tm == NTM - 1)
    def _():
        recv[0] = jnp.zeros_like(recv[0])

    body_all.wait_recv()

    @pl.when(tm < NTM - 1)
    def _():
        tail_all.wait_recv()

    total = jnp.sum(recv[0].astype(F32), axis=0) + jnp.sum(recv[1].astype(F32), axis=0)
    series = total * (1.0 / 32.0)
    series = jnp.concatenate([series, pltpu.roll(series, 4, 0)], axis=1).astype(BF16)
    turned = jnp.dot(series, analytic_ref[...], preferred_element_type=F32)
    real, imag = response[0], response[1]
    products = []
    for d in range(4):
        line_real, line_imag = turned[d : d + 1, :256], turned[d : d + 1, 256:]
        products.append(
            jnp.concatenate(
                [real * line_real - imag * line_imag, real * line_imag + imag * line_real], axis=1
            ).astype(BF16)
        )
    corr = jnp.dot(jnp.concatenate(products, axis=0), back_ref[...], preferred_element_type=F32)
    out_ref[...] = (corr[:, :128] * corr[:, :128] + corr[:, 128:] * corr[:, 128:]).astype(BF16).reshape(4, 32, 128)
    body_all.wait_send()

    @pl.when(tm > 0)
    def _():
        tail_all.wait_send()


def shards(filterbank, chan_delay, tail_len, kernels):
    vmem = pl.BlockSpec(memory_space=pltpu.VMEM)
    power = pl.pallas_call(
        kernel,
        out_shape=jax.ShapeDtypeStruct((4, 32, 128), BF16),
        in_specs=[pl.BlockSpec(memory_space=pltpu.HBM)] * 7,
        out_specs=vmem,
        scratch_shapes=[
            pltpu.VMEM((32, 256), BF16),
            pltpu.VMEM((8, 128), jnp.int32),
            pltpu.VMEM((1, 128), jnp.int32),
            pltpu.VMEM((64, 256), BF16),
            pltpu.VMEM((256, 512), BF16),
            pltpu.VMEM((512, 512), BF16),
            pltpu.VMEM((512, 256), BF16),
            pltpu.VMEM((2, 32, 256), F32),
            pltpu.SemaphoreType.DMA((7,)),
            pltpu.VMEM((296, 128), F32),
            pltpu.VMEM((288, 128), F32),
            pltpu.VMEM((544, 128), F32),
            pltpu.VMEM((16, 16, 128), F32),
            pltpu.VMEM((2, NCHAN, 8, 128), BF16),
            pltpu.VMEM((2, NCHAN, 8, 128), BF16),
            pltpu.SemaphoreType.DMA,
            pltpu.SemaphoreType.DMA((2,)),
            pltpu.SemaphoreType.REGULAR,
            pltpu.SemaphoreType.REGULAR,
            pltpu.SemaphoreType.REGULAR,
        ],
        compiler_params=pltpu.CompilerParams(
            collective_id=0, has_side_effects=True, vmem_limit_bytes=32 * 1024 * 1024
        ),
        name="dedisperse",
    )(
        *[
            pltpu.with_memory_space_constraint(a, pltpu.HBM)
            for a in (
                filterbank,
                chan_delay.reshape(8, 128),
                tail_len.reshape(1, 128),
                kernels.reshape(64, 256),
                *map(jnp.asarray, tables()),
            )
        ]
    )
    return power.transpose(1, 0, 2)


def solution(mesh):
    placed = (P("chan", "tm"), P(), P(), P())
    return jax.shard_map(
        shards, mesh=mesh, in_specs=placed, out_specs=P(None, "chan", "tm"), check_vma=False
    )
```

```python
import functools
import math

import jax
import jax.numpy as jnp
import ml_dtypes
import numpy as np
from jax import lax
from jax.experimental import pallas as pl
from jax.experimental.pallas import tpu as pltpu
from jax.sharding import PartitionSpec as P

MESH = pl.DeviceIdType.MESH
NCHAN, NTM, HALF = 32, 8, 16
F32, BF16 = jnp.float32, jnp.bfloat16

def tables():
    u = np.arange(256)
    m = np.arange(128)
    sums = np.exp(-2j * math.pi * (m[None, :] * u[:, None] % 256) / 256).sum(axis=1) / 16.0
    sums = sums[(u[:, None] + u[None, :]) % 256]
    analytic = np.concatenate([sums.real, sums.imag], axis=1).astype(ml_dtypes.bfloat16)
    angles = 2.0 * math.pi * ((u[:, None] - 128) * u[None, :] % 256) / 256
    taps = np.concatenate([np.cos(angles), np.sin(angles)], axis=1)
    high = taps.astype(ml_dtypes.bfloat16)
    low = (taps - high.astype(np.float64)).astype(ml_dtypes.bfloat16)
    angles = 2.0 * math.pi * (u[:, None] * m[None, :] % 256) / 256
    cosines, sines = np.cos(angles) / 256.0, np.sin(angles) / 256.0
    back = np.concatenate([np.concatenate([cosines, sines], 1), np.concatenate([-sines, cosines], 1)], 0)
    return analytic, np.concatenate([high, low], axis=0), back.astype(ml_dtypes.bfloat16)


def iota(shape, axis):
    return lax.broadcasted_iota(jnp.int32, shape, axis)


def kernel(
    x_hbm, delay_hbm, tail_hbm, taps_hbm, analytic_hbm, split_hbm, back_hbm, out_ref,
    x_ref, delay_ref, tail_ref, taps_ref, analytic_ref, split_ref, back_ref, response, load_sems, xpad, xgroup, acc, stage, send, recv, send_sem, recv_sems, ready_sem, go_sem,
):
    me = lax.axis_index("chan")
    tm = lax.axis_index("tm")
    before, after = lax.rem(tm + NTM - 1, NTM), lax.rem(tm + 1, NTM)

    def other(i):
        return i + (me <= i).astype(jnp.int32)

    pairs = [
        (delay_hbm, delay_ref), (tail_hbm, tail_ref), (x_hbm, x_ref), (taps_hbm, taps_ref),
        (analytic_hbm, analytic_ref), (split_hbm, split_ref), (back_hbm, back_ref),
    ]
    loads = [pltpu.make_async_copy(a, b, load_sems.at[n]) for n, (a, b) in enumerate(pairs)]
    barrier = pltpu.get_barrier_semaphore()

    def tell(sem, p, block):
        pl.semaphore_signal(sem, inc=1, device_id={"chan": p, "tm": block}, device_id_type=MESH)

    first_half, second_half = me < HALF, me >= HALF
    second = me // HALF
    not_first = (tm + NTM - 2) // (NTM - 1)
    last = tm // (NTM - 1)

    @pl.when(tm == 1)
    def _():
        tell(barrier, me, 0)

    @pl.when(first_half)
    def _():
        @pl.when(tm < NTM - 1)
        def _():
            for p in reversed(range(NCHAN)):
                tell(barrier, p, after)

        @pl.when(tm == NTM - 1)
        def _():
            for p in reversed(range(HALF, NCHAN)):
                tell(barrier, p, tm)
            for i in range(HALF - 1):
                tell(barrier, other(i), tm)

    @pl.when(second_half)
    def _():
        for p in range(HALF):
            tell(barrier, p, lax.min(tm + 1, NTM - 1))

        @pl.when(tm < NTM - 1)
        def _():
            tell(barrier, me, after)

    for load in loads:
        load.start()

    loads[0].wait()
    loads[1].wait()
    row = delay_ref[pl.ds(me // 4, 1), :].astype(F32)
    pick = iota((32, 128), 1) == iota((32, 128), 0) + 32 * lax.rem(me, 4)
    delay = jnp.sum(jnp.where(pick, row, 0.0), axis=1, keepdims=True).astype(jnp.int32)
    tails = jnp.broadcast_to(tail_ref[...], (8, 128))
    lane = iota((8, 128), 1)
    turned = pltpu.roll(tails, 64, 1)
    tails = [jnp.where(lane < 64, tails, turned)[0:1], jnp.where(lane < 64, turned, tails)[0:1]]

    loads[2].wait()
    x = x_ref[...].astype(F32)
    xt = jnp.transpose(jnp.concatenate([x, x, x, x], axis=0))
    xpad[pl.ds(0, 16), :] = jnp.zeros((16, 128), F32)
    xpad[pl.ds(16, 256), :] = xt
    xpad[pl.ds(272, 24), :] = jnp.zeros((24, 128), F32)
    group = iota((288, 128), 1) // 32
    shifted = xpad[pl.ds(0, 288), :]
    for beta in range(1, 4):
        shifted = jnp.where(group == beta, xpad[pl.ds(beta, 288), :], shifted)
    xgroup[...] = shifted
    windows = jnp.concatenate([xgroup[pl.ds(4 * j, 272), :] for j in range(4)], axis=1).astype(BF16)
    sign = (1 - 2 * lax.rem(iota((32, 256), 1), 2)).astype(F32)
    alternating = jnp.sum(x * sign, axis=1, keepdims=True)
    row_sign = (1 - 2 * lax.rem(iota((128, 128), 0), 2)).astype(F32)
    one, zero = jnp.ones((), BF16), jnp.zeros((), BF16)

    def copy_to(kind, p):
        return pltpu.make_async_remote_copy(
            send.at[kind, p], recv.at[kind, me], send_sem, recv_sems.at[kind],
            device_id={"chan": p, "tm": tm if kind else before}, device_id_type=MESH,
        )

    def send_tails(half):
        @pl.when(tm > 0)
        def _():
            for p in range(HALF * half, HALF * half + HALF):
                copy_to(0, p).start()

    def send_bodies(half):
        for i in range(HALF - 1):
            copy_to(1, other(HALF * half + i)).start()

        @pl.when(first_half if half else second_half)
        def _():
            copy_to(1, HALF if half else HALF - 1).start()

    for half in range(2):
        shifts = (delay * tails[half]) >> 12
        shift_bf = (shifts - 16 * (iota((32, 128), 1) // 64)).astype(F32).astype(BF16)

        def one_hot(a):
            return jnp.concatenate(
                [jnp.where(shift_bf == jnp.asarray(32 * a + b, BF16), one, zero) for b in range(16)], axis=0
            )

        acc[...] = jnp.zeros_like(acc)
        for pair in range(4):
            a = 2 * pair
            hot = jnp.concatenate([one_hot(a), one_hot(a + 1)], axis=1)
            part = jnp.dot(windows, hot, preferred_element_type=F32)
            acc[pl.ds(256 - 32 * a, 272), :] += part[:, :128]
            acc[pl.ds(224 - 32 * a, 272), :] += part[:, 128:]
        longest = jnp.where(shift_bf == jnp.asarray(256, BF16), one, zero)
        longest = jnp.concatenate([longest, jnp.zeros((96, 128), BF16)], axis=0)
        acc[pl.ds(0, 272), :] += jnp.dot(windows[:, :128], longest, preferred_element_type=F32)

        parity = (1 - 2 * (shifts & 1)).astype(F32)
        nyquist = jnp.sum(alternating * parity, axis=0, keepdims=True) * (1.0 / 512.0)
        slots = pl.ds(16 * half, 16)
        for q in range(4):
            odd = pltpu.roll(acc[pl.ds(32 + 128 * q, 128), :], 64, 1)
            series = acc[pl.ds(16 + 128 * q, 128), :] + odd - row_sign * nyquist
            if q < 2:
                series = jnp.where(iota((128, 128), 0) + 128 * q >= 256 - tails[half], series, 0.0)
            stage[:, pl.ds(4 * q, 4), :] = jnp.transpose(series)[:64].reshape(16, 4, 128)
        send[0, slots] = stage[:, 0:8, :].astype(BF16)
        send[1, slots] = stage[:, 8:16, :].astype(BF16)
        if half == 0:

            @pl.when(second_half)
            def _():
                pl.semaphore_wait(barrier, 1 + HALF * (not_first + last))

                @pl.when(tm > 0)
                def _():
                    tell(ready_sem, me, before)

                send_tails(0)

                @pl.when(tm < NTM - 1)
                def _():
                    pl.semaphore_wait(ready_sem, 1)

                send_bodies(0)

    @pl.when(first_half)
    def _():
        pl.semaphore_wait(barrier, 1 + (NCHAN - 1) * (not_first + last))

        @pl.when(tm > 0)
        def _():
            tell(ready_sem, me, before)

        send_tails(0)
        send_tails(1)

        @pl.when(tm < NTM - 1)
        def _():
            pl.semaphore_wait(ready_sem, 1)

        tell(go_sem, NCHAN - 4 - me + 2 * lax.rem(me, 4), tm)
        send_bodies(0)
        send_bodies(1)

    @pl.when(second_half)
    def _():
        pl.semaphore_wait(go_sem, 1)
        send_tails(1)
        send_bodies(1)

    for load in loads[3:]:
        load.wait()
    taps = taps_ref[...]
    turned = jnp.dot(taps, split_ref[0:256], preferred_element_type=F32)
    turned += jnp.dot(taps, split_ref[256:512], preferred_element_type=F32)
    response[0] = turned[:32, :256] - turned[32:, 256:]
    response[1] = turned[:32, 256:] + turned[32:, :256]
    recv[1, me] = send[1, me]

    def arrived(kind, count):
        there = recv.at[kind, pl.ds(0, count)]
        return pltpu.make_async_remote_copy(
            there, there, send_sem, recv_sems.at[kind], device_id={"chan": other(0)}, device_id_type=MESH
        )

    tail_all, body_all = arrived(0, NCHAN), arrived(1, NCHAN - 1)
    @pl.when(tm == NTM - 1)
    def _():
        recv[0] = jnp.zeros_like(recv[0])

    body_all.wait_recv()

    @pl.when(tm < NTM - 1)
    def _():
        tail_all.wait_recv()

    total = jnp.sum(recv[0].astype(F32), axis=0) + jnp.sum(recv[1].astype(F32), axis=0)
    series = total * (1.0 / 32.0)
    series = jnp.concatenate([series, pltpu.roll(series, 4, 0)], axis=1).astype(BF16)
    turned = jnp.dot(series, analytic_ref[...], preferred_element_type=F32)
    real, imag = response[0], response[1]
    products = []
    for d in range(4):
        line_real, line_imag = turned[d : d + 1, :256], turned[d : d + 1, 256:]
        products.append(
            jnp.concatenate(
                [real * line_real - imag * line_imag, real * line_imag + imag * line_real], axis=1
            ).astype(BF16)
        )
    corr = jnp.dot(jnp.concatenate(products, axis=0), back_ref[...], preferred_element_type=F32)
    out_ref[...] = (corr[:, :128] * corr[:, :128] + corr[:, 128:] * corr[:, 128:]).astype(BF16).reshape(4, 32, 128)
    body_all.wait_send()

    @pl.when(tm > 0)
    def _():
        tail_all.wait_send()


def shards(filterbank, chan_delay, tail_len, kernels):
    vmem = pl.BlockSpec(memory_space=pltpu.VMEM)
    power = pl.pallas_call(
        kernel,
        out_shape=jax.ShapeDtypeStruct((4, 32, 128), BF16),
        in_specs=[pl.BlockSpec(memory_space=pltpu.HBM)] * 7,
        out_specs=vmem,
        scratch_shapes=[
            pltpu.VMEM((32, 256), BF16),
            pltpu.VMEM((8, 128), jnp.int32),
            pltpu.VMEM((1, 128), jnp.int32),
            pltpu.VMEM((64, 256), BF16),
            pltpu.VMEM((256, 512), BF16),
            pltpu.VMEM((512, 512), BF16),
            pltpu.VMEM((512, 256), BF16),
            pltpu.VMEM((2, 32, 256), F32),
            pltpu.SemaphoreType.DMA((7,)),
            pltpu.VMEM((296, 128), F32),
            pltpu.VMEM((288, 128), F32),
            pltpu.VMEM((544, 128), F32),
            pltpu.VMEM((16, 16, 128), F32),
            pltpu.VMEM((2, NCHAN, 8, 128), BF16),
            pltpu.VMEM((2, NCHAN, 8, 128), BF16),
            pltpu.SemaphoreType.DMA,
            pltpu.SemaphoreType.DMA((2,)),
            pltpu.SemaphoreType.REGULAR,
            pltpu.SemaphoreType.REGULAR,
        ],
        compiler_params=pltpu.CompilerParams(
            collective_id=0, has_side_effects=True, vmem_limit_bytes=32 * 1024 * 1024
        ),
        name="dedisperse",
    )(
        *[
            pltpu.with_memory_space_constraint(a, pltpu.HBM)
            for a in (
                filterbank,
                chan_delay.reshape(8, 128),
                tail_len.reshape(1, 128),
                kernels.reshape(64, 256),
                *map(jnp.asarray, tables()),
            )
        ]
    )
    return power.transpose(1, 0, 2)


def solution(mesh):
    placed = (P("chan", "tm"), P(), P(), P())
    return jax.shard_map(
        shards, mesh=mesh, in_specs=placed, out_specs=P(None, "chan", "tm"), check_vma=False
    )
```
